32 devices in a mesh: member: 2 (over x), lat: 8 (over z, y), lon: 2 (over core).
Axes of the slice: x: 2, y: 2, z: 4, core: 2. Of those that a mesh axis runs over, the one named last changes fastest.
Arguments:
- tokens: bfloat16 [128, 192, 1024], P(('member', 'lat'), 'lon'), parts along dimension 0, may hold values from -6 to 6
- ln_gain: float32 [1024], replicated, may hold values from 0.5 to 1.5
- w_query: bfloat16 [1024, 1024], replicated, may hold values from -3 to 3
- w_keyval: bfloat16 [1024, 2048], replicated, may hold values from -3 to 3
- w_out: bfloat16 [1024, 1024], replicated, may hold values from -0.1875 to 0.1875
- w_dec: bfloat16 [1024, 512], replicated, may hold values from -0.1875 to 0.1875
- nudge: float32 [32], replicated, may hold values from 0.2 to 1
- state: float32 [32, 512, 768], P(None, ('member', 'lat'), 'lon'), parts along dimension 1, may hold values from -6 to 6
Outputs:
- advanced: float32 [32, 512, 768], P(None, ('member', 'lat', 'lon')), parts along dimension 1
The draws below stay inside these ranges and needn't reach their ends.
There are 2 independent parts, one for each index of `member`. The reference program is written for one: setup_inputs(seed, part) draws one part's arguments, and reference() takes and returns one part's arrays. A program takes and returns all parts, laid end to end along the dimension named above; an argument that names none is the same for every part. Nothing has to cross between parts.
All inputs are finite; a program needn't handle non-finite values.
Results may differ from the reference program's by a relative error of at most 0.003.
Values may be sent and summed in bfloat16 or wider, within the bound.
A program may use at most 128 MiB of HBM per device.

```python
import math
import jax
import jax.numpy as jnp
from jax import lax

D = 1024
HEADS = 16
WIN = 8
PATCH = 4
VARS = 4
LEV = 8
LON_PIX = 768
KEEP = 256
CH = 32
NTR = 64
NTC = 192
NLAT_PIX = 256


def paired_weights(key):
    base_key = jax.random.fold_in(key, 1234)
    key_keys, key_query = jax.random.split(base_key, 2)
    keyval_raw = jax.random.normal(key_keys, (D, 2 * D), jnp.float32) / math.sqrt(D)
    query_raw = jax.random.normal(key_query, (D, D), jnp.float32) / math.sqrt(D)
    return (jnp.clip(query_raw, -3.0, 3.0), jnp.clip(keyval_raw, -3.0, 3.0))


def draw_w_query(key, part):
    return paired_weights(key)[0].astype(jnp.bfloat16)


def draw_w_keyval(key, part):
    return paired_weights(key)[1].astype(jnp.bfloat16)


def block_scale(key, dims, pieces, least, largest):
    def one(axis_at, parts):
        heights = jax.random.uniform(jax.random.fold_in(jax.random.fold_in(key, 6), axis_at), (parts,), jnp.float32, least / len(pieces), largest / len(pieces))
        return jnp.repeat(jnp.exp(heights), dims[axis_at] // parts).reshape((-1,) + (1,) * (len(dims) - axis_at - 1))

    gain = one(*pieces[0])
    for cut in pieces[1:]:
        gain = gain * one(*cut)
    return gain


def normal_values(own_key, shape, deviation, limit, cuts=(), held_as=jnp.bfloat16):
    result = jax.random.normal(own_key, shape, jnp.float32) * deviation
    if len(cuts) > 0:
        result = block_scale(own_key, shape, cuts, -0.22, 0.18) * result
    return jnp.clip(result, min=-limit, max=limit).astype(held_as)


def setup_inputs(seed: int = 0, part: int = 0) -> dict:
    splits = jax.random.split(jax.random.key(seed), 9)
    part_keys = jax.random.split(jax.random.fold_in(splits[8], part), 9)
    return {
        "tokens": normal_values(part_keys[0], (NTR, NTC, D), 1.0, 6.0, ((0, 8), (1, 2))),
        "ln_gain": jnp.clip(1.0 + 0.1 * jax.random.normal(splits[1], (D,), jnp.float32), 0.5, 1.5),
        "w_query": draw_w_query(jax.random.fold_in(splits[8], 71), part),
        "w_keyval": draw_w_keyval(jax.random.fold_in(splits[8], 71), part),
        "w_out": normal_values(splits[4], (D, D), D ** -0.5, 0.1875),
        "w_dec": normal_values(splits[5], (D, CH * PATCH * PATCH), D ** -0.5, 0.1875),
        "nudge": jnp.clip(jnp.exp(jax.random.uniform(splits[6], (CH,), jnp.float32, math.log(0.2), math.log(1.0))), 0.2, 1.0),
        "state": normal_values(part_keys[7], (CH, NLAT_PIX, LON_PIX), 1.0, 6.0, ((1, 8), (2, 2)), jnp.float32),
    }


time_step = 0.1
diffusion = 0.5
epsilon = 1e-05

def layer_norm(inputs, gain_vector):
    centred = inputs - lax.optimization_barrier(jnp.mean(inputs, axis=-1, keepdims=True))
    variance = lax.optimization_barrier(jnp.mean(centred * centred, axis=-1, keepdims=True))
    return (centred * lax.rsqrt(variance + epsilon) * gain_vector).astype(jnp.bfloat16)

def to_windows(tensor, row_blocks, col_blocks):
    features = tensor.shape[-1]
    shaped = tensor.reshape(row_blocks, WIN, col_blocks, WIN, features)
    return shaped.transpose(0, 2, 1, 3, 4).reshape(row_blocks * col_blocks, WIN * WIN, features)

def from_windows(tensor, row_blocks, col_blocks):
    features = tensor.shape[-1]
    shaped = tensor.reshape(row_blocks, col_blocks, WIN, WIN, features)
    return shaped.transpose(0, 2, 1, 3, 4).reshape(row_blocks * WIN, col_blocks * WIN, features)

def window_attention(queries, keys_win, values_win, key_valid):
    windows_count, window_cells, model_width = queries.shape
    head_size = model_width // HEADS
    query_heads = queries.astype(jnp.float32).reshape(windows_count, window_cells, HEADS, head_size)
    key_heads = keys_win.astype(jnp.float32).reshape(windows_count, window_cells, HEADS, head_size)
    value_heads = values_win.astype(jnp.float32).reshape(windows_count, window_cells, HEADS, head_size)
    scores = jnp.einsum('wqhd,wkhd->whqk', query_heads, key_heads) / math.sqrt(head_size)
    scores = jnp.where(key_valid[:, None, None, :], scores, -1e+30)
    peak_score = lax.optimization_barrier(jnp.max(scores, axis=-1, keepdims=True))
    weights = jnp.exp(scores - peak_score)
    weights = (weights / lax.optimization_barrier(jnp.sum(weights, axis=-1, keepdims=True))).astype(jnp.bfloat16)
    weights = lax.optimization_barrier(weights).astype(jnp.float32)
    mixed_out = jnp.einsum('whqk,wkhd->wqhd', weights, value_heads)
    return mixed_out.astype(jnp.bfloat16).reshape(windows_count, window_cells, model_width)

def zonal_basis(length, kept_waves):
    columns = jnp.arange(length, dtype=jnp.int32)
    wave_index = jnp.arange(kept_waves, dtype=jnp.int32)
    winding = columns[:, None] * wave_index[None, :] % length
    phases = winding.astype(jnp.float32) * (2.0 * math.pi / length)
    basis_table = jnp.concatenate([jnp.cos(phases), jnp.sin(phases)], axis=1)
    factor = jnp.where(wave_index == 0, 1.0, 2.0).astype(jnp.float32) / length
    return (basis_table, jnp.concatenate([factor, factor]))

def tendency(padded):
    centre = padded[:, 1:-1, 1:-1]
    east_cell = padded[:, 1:-1, 2:]
    west_cell = padded[:, 1:-1, :-2]
    north_cell = padded[:, 2:, 1:-1]
    south_cell = padded[:, :-2, 1:-1]
    field_shape = (VARS, LEV) + centre.shape[1:]
    wind_u = centre[:LEV][None]
    wind_v = centre[LEV:2 * LEV][None]
    advection = wind_u * (east_cell - west_cell).reshape(field_shape) * 0.5
    advection = advection + wind_v * (north_cell - south_cell).reshape(field_shape) * 0.5
    spread_term = diffusion * (east_cell + west_cell + north_cell + south_cell - 4.0 * centre)
    return spread_term - advection.reshape(centre.shape)

def extend_full(field):
    padded_rows = jnp.pad(field, ((0, 0), (1, 1), (0, 0)))
    return jnp.concatenate([padded_rows[..., -1:], padded_rows, padded_rows[..., :1]], axis=2)

def reference(tokens, ln_gain, w_query, w_keyval, w_out, w_dec, nudge, state):
    rows_all, cols_all, model_width = tokens.shape
    half_win = WIN // 2
    padded = jnp.pad(tokens, ((half_win, half_win), (0, 0), (0, 0)))
    padded = jnp.roll(padded, half_win, axis=1)
    inside = jnp.pad(jnp.ones((rows_all,), jnp.int32), (half_win, half_win))
    col_blocks = cols_all // WIN

    def one_band(band_index):
        row_start = (band_index * WIN).astype(jnp.int32)
        token_band = lax.dynamic_slice_in_dim(padded, row_start, WIN, 0)
        row_keep = lax.dynamic_slice_in_dim(inside, row_start, WIN, 0)
        normed = layer_norm(token_band.astype(jnp.float32), ln_gain)
        flat_rows = normed.reshape(WIN * cols_all, model_width)
        queries = jnp.dot(flat_rows, w_query, preferred_element_type=jnp.float32).astype(jnp.bfloat16)
        keyval = jnp.dot(flat_rows, w_keyval, preferred_element_type=jnp.float32).astype(jnp.bfloat16)
        queries = queries.reshape(WIN, cols_all, model_width)
        keyval = keyval.reshape(WIN, cols_all, 2 * model_width)
        keep_grid = jnp.broadcast_to(row_keep[:, None, None], (WIN, cols_all, 1))
        key_valid = to_windows(keep_grid, 1, col_blocks)[..., 0] > 0
        keyval_win = to_windows(keyval, 1, col_blocks)
        outputs = window_attention(to_windows(queries, 1, col_blocks), keyval_win[..., :model_width], keyval_win[..., model_width:], key_valid)
        return from_windows(outputs, 1, col_blocks)
    all_bands = lax.map(one_band, jnp.arange(rows_all // WIN + 1, dtype=jnp.int32))
    attended = all_bands.reshape(rows_all + WIN, cols_all, model_width)[half_win:half_win + rows_all]
    attended = jnp.roll(attended, -half_win, axis=1)
    update = jnp.dot(attended.reshape(-1, model_width), w_out, preferred_element_type=jnp.float32)
    layer_out = (tokens.astype(jnp.float32).reshape(-1, model_width) + update).astype(jnp.bfloat16)
    decoded = jnp.dot(layer_out, w_dec, preferred_element_type=jnp.float32)
    decoded = decoded.reshape(rows_all, cols_all, VARS * LEV, PATCH, PATCH).transpose(2, 0, 3, 1, 4)
    decoded = decoded.reshape(VARS * LEV, rows_all * PATCH, cols_all * PATCH)
    basis_table, factor = zonal_basis(LON_PIX, KEEP)
    difference = (decoded - state).reshape(-1, LON_PIX)
    coefficients = jnp.dot(difference, basis_table, precision=lax.Precision.HIGHEST, preferred_element_type=jnp.float32)
    filtered = jnp.dot(coefficients * factor, basis_table.T, precision=lax.Precision.HIGHEST, preferred_element_type=jnp.float32)
    nudged = state + nudge[:, None, None] * filtered.reshape(state.shape)
    first_section = nudged + time_step * tendency(extend_full(nudged))
    return 0.5 * (nudged + first_section + time_step * tendency(extend_full(first_section)))
```

```python
import functools
import math

import jax
import jax.numpy as jnp
import ml_dtypes
import numpy as np
from jax import lax
from jax.experimental import pallas as pl
from jax.experimental.pallas import tpu as pltpu
from jax.sharding import PartitionSpec as P

HEADS = 16
WIN = 8
PATCH = 4
VARS = 4
LEV = 8
KEEP = 256

time_step = 0.1
diffusion = 0.5
epsilon = 1e-05
F32 = jnp.float32
BF16 = jnp.bfloat16
NT = (((1,), (1,)), ((), ()))


def full_spec(shape):
    zeros = (0,) * len(shape)
    return pl.BlockSpec(shape, lambda *_: zeros, pipeline_mode=pl.Buffered(1))


def filter_tables(length, kept):
    offset = np.arange(length)
    waves = np.arange(1, kept)
    kernel = (1.0 + 2.0 * np.cos(2.0 * np.pi * ((offset[:, None] * waves[None, :]) % length) / length).sum(1)) / length
    table = kernel[(offset[None, :] - offset[:, None]) % length].astype(np.float32)
    high = table.astype(ml_dtypes.bfloat16)
    low = (table - high.astype(np.float32)).astype(ml_dtypes.bfloat16)
    return high, low


def layer_kernel(sizes, valid_ref, gain_ref, wq_ref, wkv_ref, wo_ref, wd_ref, *rest):
    rows, cols, cw = sizes
    x_refs, (dec_ref, att, lo) = rest[:-3], rest[-3:]
    step = pl.program_id(0)
    width = wq_ref.shape[0]
    nw = cw // WIN
    cells = rows * WIN
    parts = [r[...].astype(F32).reshape(r.shape[0], nw, WIN, width) for r in x_refs]
    x = parts[0] if len(parts) == 1 else jnp.concatenate(parts, axis=0)
    x = jnp.swapaxes(x, 0, 1).reshape(nw * cells, width)
    centred = x - jnp.mean(x, axis=-1, keepdims=True)
    variance = jnp.mean(centred * centred, axis=-1, keepdims=True)
    normed = (centred * lax.rsqrt(variance + epsilon) * gain_ref[...]).astype(BF16)
    head = width // HEADS
    q = jnp.dot(normed, wq_ref[...], preferred_element_type=F32).astype(BF16)
    q = q * jnp.asarray(1.0 / math.sqrt(head), BF16)
    kv = jnp.dot(normed, wkv_ref[...], preferred_element_type=F32).astype(BF16)
    pair = 2 * head
    lane = lax.broadcasted_iota(jnp.int32, (cells, pair), 1)
    first = lane < head
    key = lax.broadcasted_iota(jnp.int32, (1, cells), 1)
    if len(parts) > 1:
        bias = jnp.where((key < cells // 2) & (valid_ref[0] == 0), -1e30, 0.0).astype(F32)
    else:
        bias = None
    for w in range(nw):
        at = slice(w * cells, (w + 1) * cells)
        for p in range(HEADS // 2):
            on = slice(p * pair, (p + 1) * pair)
            on_v = slice(width + p * pair, width + (p + 1) * pair)
            qp = q[at, on]
            zero = jnp.zeros_like(qp)
            q2 = jnp.concatenate([jnp.where(first, qp, zero), jnp.where(first, zero, qp)], axis=0)
            s = lax.dot_general(q2, kv[at, on], NT, preferred_element_type=F32)
            if bias is not None:
                s = s + bias
            e = jnp.exp(s - jnp.max(s, axis=-1, keepdims=True))
            e = (e * (1.0 / jnp.sum(e, axis=-1, keepdims=True))).astype(BF16)
            o = jnp.dot(e, kv[at, on_v], preferred_element_type=F32)
            att[at, on] = jnp.where(first, o[:cells], o[cells:]).astype(BF16)
    out = x + jnp.dot(att[...], wo_ref[...], preferred_element_type=F32)
    out = jnp.swapaxes(out.reshape(nw, rows, WIN, width), 0, 1).reshape(rows, cw, width).astype(BF16)
    for r in range(rows):
        lo[pl.ds(pl.multiple_of(r * cols + step * cw, cw), cw), :] = out[r]

    @pl.when(step == cols // cw - 1)
    def _():
        dec_ref[...] = lax.dot_general(wd_ref[...], lo[...], NT, preferred_element_type=F32).astype(BF16)


def window_layer(valid, gain, wq, wkv, wo, wd, *blocks):
    rows = sum(b.shape[0] for b in blocks)
    cols, width = blocks[0].shape[1:]
    cw = math.gcd(cols, 32)
    grid = (cols // cw,)
    tokens = rows * cols
    flops = 2 * tokens * width * (4 * width + wd.shape[0])
    return pl.pallas_call(
        functools.partial(layer_kernel, (rows, cols, cw)),
        grid=grid,
        out_shape=jax.ShapeDtypeStruct((wd.shape[0], tokens), BF16),
        in_specs=[
            pl.BlockSpec(memory_space=pltpu.SMEM),
            full_spec(gain.shape),
            full_spec(wq.shape),
            full_spec(wkv.shape),
            full_spec(wo.shape),
            full_spec(wd.shape),
        ]
        + [pl.BlockSpec((b.shape[0], cw, width), lambda i: (0, i, 0)) for b in blocks],
        out_specs=pl.BlockSpec((wd.shape[0], tokens), lambda i: (0, 0)),
        scratch_shapes=[
            pltpu.VMEM((rows * cw, width), BF16),
            pltpu.VMEM((tokens, width), BF16),
        ],
        cost_estimate=pl.CostEstimate(flops=flops * 2, bytes_accessed=12 * width * width, transcendentals=0),
        compiler_params=pltpu.CompilerParams(vmem_limit_bytes=60 * 2**20),
        name="window_layer",
    )(valid, gain, wq, wkv, wo, wd, *blocks)


def state_kernel(state_ref, nudge_ref, high_ref, low_ref, base_ref):
    rows, channels, length = state_ref.shape
    for y in range(0, rows, PATCH):
        s = state_ref[y : y + PATCH].reshape(PATCH * channels, length)
        s_high = s.astype(BF16)
        s_low = (s - s_high.astype(F32)).astype(BF16)
        kept = jnp.dot(s_high, high_ref[...], preferred_element_type=F32)
        kept = kept + jnp.dot(s_low, high_ref[...], preferred_element_type=F32)
        kept = kept + jnp.dot(s_high, low_ref[...], preferred_element_type=F32)
        kept = kept.reshape(PATCH, channels, length)
        base_ref[y : y + PATCH] = state_ref[y : y + PATCH] - nudge_ref[...][None] * kept


def decoded_kernel(base_ref, d0_ref, d1_ref, nudge_ref, high_ref, low_ref, out_ref):
    rows, channels, length = base_ref.shape
    cols = length // PATCH // 2
    part = PATCH * channels
    for r in range(rows // PATCH):
        pieces = []
        for b in range(PATCH):
            for d in (d0_ref, d1_ref):
                pieces.append(d[b * part : (b + 1) * part, r * cols : (r + 1) * cols])
        x = jnp.concatenate(pieces, axis=1)
        kept = jnp.dot(x, high_ref[...], preferred_element_type=F32)
        kept = kept + jnp.dot(x, low_ref[...], preferred_element_type=F32)
        kept = kept.reshape(PATCH, channels, length)
        y = r * PATCH
        out_ref[y : y + PATCH] = base_ref[y : y + PATCH] + nudge_ref[...][None] * kept


def tendency_row(south, centre, north):
    channels, length = centre.shape
    west = pltpu.roll(centre, 1, 1)
    east = pltpu.roll(centre, length - 1, 1)
    u = centre[:LEV][None]
    v = centre[LEV : 2 * LEV][None]
    dx = (east - west).reshape(VARS, LEV, length)
    dy = (north - south).reshape(VARS, LEV, length)
    advection = ((u * dx + v * dy) * 0.5).reshape(channels, length)
    return diffusion * (east + west + north + south - 4.0 * centre) - advection


def section_kernel(inside_ref, field_ref, before_ref, after_ref, out_ref, first):
    rows = field_ref.shape[0]

    def row(y):
        if y < 0:
            return before_ref[y + 2].astype(F32)
        if y >= rows:
            return after_ref[y - rows].astype(F32)
        return field_ref[y]

    for y in range(-1, rows + 1):
        value = row(y) + time_step * tendency_row(row(y - 1), row(y), row(y + 1))
        if y == -1:
            value = value * inside_ref[0]
        if y == rows:
            value = value * inside_ref[1]
        first[y + 1] = value
    for y in range(rows):
        second = tendency_row(first[y], first[y + 1], first[y + 2])
        out_ref[y] = 0.5 * (field_ref[y] + first[y + 1] + time_step * second)


def body(tokens, ln_gain, w_query, w_keyval, w_out, w_dec, nudge, state):
    half = WIN // 2
    tok_rows, tok_cols, width = tokens.shape
    n_lat, n_lon = lax.axis_size("lat"), lax.axis_size("lon")
    lat, lon = lax.axis_index("lat"), lax.axis_index("lon")
    channels = nudge.shape[0]
    length = state.shape[2] * n_lon
    band = state.shape[1] // n_lon
    lat_up = [(i, i + 1) for i in range(n_lat - 1)]
    swap = [(i, (i + 1) % n_lon) for i in range(n_lon)]

    raw_top = lax.ppermute(tokens[half:], "lat", lat_up)
    edge = lax.ppermute(tokens[:, :half], "lon", [(j, i) for i, j in swap])
    edge_top = lax.ppermute(edge[half:], "lat", lat_up)
    own = jnp.concatenate([tokens[:, half:], edge], axis=1)
    top = jnp.concatenate([raw_top[:, half:], edge_top], axis=1)

    wd = w_dec.reshape(width, channels, PATCH, PATCH).transpose(3, 2, 1, 0).reshape(-1, width)
    gain = ln_gain[None]
    valid = (lat > 0).astype(jnp.int32)[None]
    weights = (valid, gain, w_query, w_keyval, w_out, wd)

    is_low = lon == 0
    mine = jnp.where(is_low, state[:, :band], state[:, band:])
    other = jnp.where(is_low, state[:, band:], state[:, :band])
    other = lax.ppermute(other, "lon", swap)
    band_state = jnp.concatenate(
        [jnp.where(is_low, mine, other), jnp.where(is_low, other, mine)], axis=2
    ).transpose(1, 0, 2)
    high, low = filter_tables(length, KEEP)
    high, low = jnp.asarray(high), jnp.asarray(low)
    strength = nudge[:, None]
    field = jax.ShapeDtypeStruct((band, channels, length), F32)
    limit = pltpu.CompilerParams(vmem_limit_bytes=48 * 2**20)
    matmul = 2 * band * channels * length * length
    base = pl.pallas_call(
        state_kernel,
        out_shape=field,
        compiler_params=limit,
        cost_estimate=pl.CostEstimate(flops=3 * matmul, bytes_accessed=2**22, transcendentals=0),
        name="state_filter",
    )(band_state, strength, high, low)
    bottom_dec = window_layer(*weights, own[half:])

    dec = window_layer(*weights, top, own[:half])
    dec_top, dec_own = dec[:, : half * tok_cols], dec[:, half * tok_cols :]
    axes = ("lat", "lon")
    last_lon = n_lon - 1

    def flat(i, j):
        return i * n_lon + j

    to_last = [
        lax.ppermute(dec_top, axes, [(flat(i + 1, j), flat(i, last_lon)) for i in range(n_lat - 1)])
        for j in range(n_lon)
    ]
    across = lax.ppermute(jnp.where(is_low, bottom_dec, dec_own), "lon", swap)
    last = lat == n_lat - 1
    d0 = jnp.where(is_low, dec_own, jnp.where(last, across, to_last[0]))
    d1 = jnp.where(is_low, across, jnp.where(last, bottom_dec, to_last[1]))

    def decoder_rows(table):
        shaped = jnp.roll(table.reshape(-1, PATCH, length), -half, axis=0)
        return shaped.transpose(1, 0, 2).reshape(length, length)

    nudged = pl.pallas_call(
        decoded_kernel,
        out_shape=field,
        compiler_params=limit,
        cost_estimate=pl.CostEstimate(flops=2 * matmul, bytes_accessed=2**22, transcendentals=0),
        name="decoded_filter",
    )(base, d0, d1, strength, decoder_rows(high), decoder_rows(low))

    bands = n_lat * n_lon
    up = [(i, i + 1) for i in range(bands - 1)]
    down = [(j, i) for i, j in up]
    before = lax.ppermute(nudged[-2:].astype(BF16), axes, up)
    after = lax.ppermute(nudged[:2].astype(BF16), axes, down)
    place = lat * n_lon + lon
    inside = jnp.stack([place > 0, place < bands - 1]).astype(F32)
    advanced = pl.pallas_call(
        section_kernel,
        out_shape=field,
        in_specs=[pl.BlockSpec(memory_space=pltpu.SMEM)] + [pl.BlockSpec(memory_space=pltpu.VMEM)] * 3,
        scratch_shapes=[pltpu.VMEM((band + 2, channels, length), F32)],
        compiler_params=limit,
        name="two_sections",
    )(inside, nudged, before, after)
    return advanced.transpose(1, 0, 2)


def solution(mesh):
    in_specs = (
        P(("member", "lat"), "lon", None),
        P(),
        P(),
        P(),
        P(),
        P(),
        P(),
        P(None, ("member", "lat"), "lon"),
    )
    out_specs = P(None, ("member", "lat", "lon"), None)
    return jax.shard_map(body, mesh=mesh, in_specs=in_specs, out_specs=out_specs, check_vma=False)
```

```python
import functools
import math

import jax
import jax.numpy as jnp
import numpy as np
from jax import lax
from jax.experimental import pallas as pl
from jax.experimental.pallas import tpu as pltpu
from jax.sharding import PartitionSpec as P

HEADS = 16
WIN = 8
PATCH = 4
VARS = 4
LEV = 8
KEEP = 256

time_step = 0.1
diffusion = 0.5
epsilon = 1e-05
F32 = jnp.float32
BF16 = jnp.bfloat16
NT = (((1,), (1,)), ((), ()))


def filter_rows(length, kept, stride):
    offset = np.arange(length)
    waves = np.arange(1, kept)
    angles = 2.0 * np.pi * ((offset[:, None] * waves[None, :]) % length) / length
    kernel = (1.0 + 2.0 * np.cos(angles).sum(1)) / length
    return kernel[(offset[None, :] - stride * np.arange(16)[:, None]) % length].astype(np.float32)


def split(value):
    high = value.astype(BF16)
    return high, (value - high.astype(F32)).astype(BF16)


def cycle_kernel(
    n_lat, tokens, state, wq_hbm, wkv_hbm, wo_hbm, wd_hbm, gain_ref, nudge_ref, rows1_ref, rows4_ref, out_ref,
    wqkv, wo, wd, wdt, own, recv, edge, corner, xs, xs_b, normed, qkv, qkv_b, att, lo,
    band, base, high, low, dhigh, dlow, d0, d1, send_top, send_side, up_rows, down_rows, before, after, first,
    load_sem, send_sem, recv_sem,
):
    lat, lon = lax.axis_index("lat"), lax.axis_index("lon")
    half = WIN // 2
    cols, width = tokens.shape[1:]
    windows = cols // WIN
    strip = edge.shape[1]
    tall, channels, length = base.shape
    wide = state.shape[2]
    is_low, is_high = lon == 0, lon == 1
    has_prev, has_next = lat > 0, lat < n_lat - 1
    prev, nxt = jnp.maximum(lat - 1, 0), jnp.minimum(lat + 1, n_lat - 1)
    peer = 1 - lon

    def load(i, src, dst):
        return pltpu.make_async_copy(src, dst, load_sem.at[i])

    def remote(i, src, dst, to_lat, to_lon):
        return pltpu.make_async_remote_copy(
            src_ref=src, dst_ref=dst, send_sem=send_sem.at[i], recv_sem=recv_sem.at[i],
            device_id={"lat": to_lat, "lon": to_lon}, device_id_type=pl.DeviceIdType.MESH,
        )

    own_load = load(0, tokens, own)
    loads = [
        load(1, wq_hbm, wqkv.at[:, pl.ds(0, width)]),
        load(2, wkv_hbm, wqkv.at[:, pl.ds(width, 2 * width)]),
        load(3, wo_hbm, wo),
        load(4, wd_hbm, wd),
    ]
    my_rows = pl.ds(pl.multiple_of(lon * tall, 8), tall)
    peer_rows = pl.ds(pl.multiple_of(peer * tall, 8), tall)
    my_cols = pl.ds(pl.multiple_of(lon * wide, 128), wide)
    own_state = load(5, state.at[:, my_rows, :], band.at[:, :, my_cols])
    own_load.start()
    for item in loads:
        item.start()
    own_state.start()

    barrier = pltpu.get_barrier_semaphore()

    def greet(to_lat, to_lon):
        pl.semaphore_signal(
            barrier, inc=1, device_id={"lat": to_lat, "lon": to_lon}, device_id_type=pl.DeviceIdType.MESH
        )

    greet(lat, peer)

    @pl.when(has_prev)
    def _():
        greet(prev, lon)
        greet(prev, peer)

    @pl.when(has_next)
    def _():
        greet(nxt, lon)
        greet(nxt, peer)

    pl.semaphore_wait(barrier, 1 + 2 * has_prev.astype(jnp.int32) + 2 * has_next.astype(jnp.int32))

    row_a = remote(0, tokens.at[pl.ds(half, half), pl.ds(0, strip), :], recv.at[:, pl.ds(0, strip), :], nxt, lon)
    row_b = remote(
        1, tokens.at[pl.ds(half, half), pl.ds(strip, cols - strip), :],
        recv.at[:, pl.ds(strip, cols - strip), :], nxt, lon,
    )
    edge_copy = remote(2, tokens.at[:, pl.ds(0, strip), :], edge, lat, peer)
    state_copy = remote(3, state.at[:, peer_rows, :], band.at[:, :, my_cols], lat, peer)
    corner_copy = remote(4, recv.at[:, pl.ds(0, strip), :], corner, lat, peer)

    @pl.when(has_next)
    def _():
        row_a.start()
        row_b.start()

    edge_copy.start()
    state_copy.start()

    def project(block, strip_block, x_out, qkv_out, at):
        for r in range(half):
            row = block[r].astype(F32)
            side = strip_block[r].astype(F32)
            row = jnp.concatenate([row[half:], side[:half]], axis=0)
            centred = row - jnp.mean(row, axis=-1, keepdims=True)
            variance = jnp.mean(centred * centred, axis=-1, keepdims=True)
            unit = centred * lax.rsqrt(variance + epsilon) * gain_ref[...]
            x_out[r] = row.reshape(windows, WIN, width)
            normed[r] = unit.reshape(windows, WIN, width)
        flat = jnp.swapaxes(normed[...], 0, 1).reshape(windows * half * WIN, width).astype(BF16)
        scale = jnp.float32(1.0 / math.sqrt(width // HEADS))

        @pl.loop(0, 3 * width // 256)
        def _(n):
            on = pl.ds(pl.multiple_of(n * 256, 256), 256)
            value = jnp.dot(flat, wqkv[:, on], preferred_element_type=F32).astype(BF16)
            value = (value.astype(F32) * jnp.where(n < width // 256, scale, 1.0)).astype(BF16)
            qkv_out[:, at, on] = value.reshape(windows, half * WIN, 256)

    def attend(qkv_in, cells, bias):
        head = width // HEADS
        pair = 2 * head
        lanes = lax.broadcasted_iota(jnp.int32, (cells, pair), 1) < head

        @pl.loop(0, windows)
        def _(w):
            for p in range(HEADS // 2):
                on = p * pair
                qp = qkv_in[w, :, on : on + pair]
                zero = jnp.zeros_like(qp)
                q2 = jnp.concatenate([jnp.where(lanes, qp, zero), jnp.where(lanes, zero, qp)], axis=0)
                kp = qkv_in[w, :, width + on : width + on + pair]
                vp = qkv_in[w, :, 2 * width + on : 2 * width + on + pair]
                s = lax.dot_general(q2, kp, NT, preferred_element_type=F32)
                if bias is not None:
                    s = s + bias
                e = jnp.exp(s - jnp.max(s, axis=-1, keepdims=True))
                e = (e * (1.0 / jnp.sum(e, axis=-1, keepdims=True))).astype(BF16)
                o = jnp.dot(e, vp, preferred_element_type=F32)
                att[w, 0:cells, on : on + pair] = jnp.where(lanes, o[:cells], o[cells:]).astype(BF16)

    def decode(at, x_in, outs):
        mixed = att[:, at, :].reshape(windows * half * WIN, width)

        @pl.loop(0, width // 256)
        def _(n):
            on = pl.ds(pl.multiple_of(n * 256, 256), 256)
            update = jnp.dot(mixed, wo[:, on], preferred_element_type=F32)
            update = jnp.swapaxes(update.reshape(windows, half, WIN, 256), 0, 1)
            value = x_in[:, :, :, on] + update
            lo[:, on] = value.reshape(half * cols, 256).astype(BF16)

        value = lax.dot_general(wdt[...], lo[...], NT, preferred_element_type=F32).astype(BF16)
        for chosen_here, out in outs:
            if chosen_here is None:
                out[...] = value
            else:

                @pl.when(chosen_here)
                def _():
                    out[...] = value

    top_at, own_at = slice(0, half * WIN), slice(half * WIN, 2 * half * WIN)
    x_top, x_own = xs.at[0], xs.at[1]
    own_load.wait()
    edge_copy.wait()
    loads[0].wait()
    loads[1].wait()
    project(own.at[pl.ds(0, half)], edge.at[pl.ds(0, half)], x_own, qkv, own_at)

    loads[2].wait()
    loads[3].wait()
    patches = wdt.shape[0]
    row_id = lax.broadcasted_iota(jnp.int32, (patches, patches), 0)
    col_id = lax.broadcasted_iota(jnp.int32, (patches, patches), 1)
    area = PATCH * PATCH
    wanted = (row_id % channels) * area + (row_id // channels) % PATCH * PATCH + row_id // (PATCH * channels)
    chosen = (col_id == wanted).astype(F32).astype(BF16)
    wdt[...] = lax.dot_general(chosen, wd[...], NT, preferred_element_type=F32).astype(BF16)

    @pl.when(lat == n_lat - 1)
    def _():
        project(own.at[pl.ds(half, half)], edge.at[pl.ds(half, half)], xs_b, qkv_b, top_at)
        attend(qkv_b, half * WIN, None)
        decode(top_at, xs_b, [(is_high, d1), (is_low, send_side)])

    blocks = length // 16

    @pl.loop(0, blocks)
    def _(g):
        on = pl.ds(pl.multiple_of(g * 16, 16), 16)
        high[on, :], low[on, :] = split(pltpu.roll(rows1_ref[...], g * 16, 1))
        per = blocks // PATCH
        shift = lax.rem((lax.rem(g, per) * 16 + half) * PATCH + g // per, length)
        dhigh[on, :], dlow[on, :] = split(pltpu.roll(rows4_ref[...], shift, 1))

    own_state.wait()
    state_copy.wait()

    @pl.loop(0, channels // LEV)
    def _(g):
        on = pl.ds(pl.multiple_of(g * LEV, LEV), LEV)
        s = band[on].reshape(LEV * tall, length)
        s_high, s_low = split(s)
        kept = jnp.dot(s_high, high[...], preferred_element_type=F32)
        kept = kept + jnp.dot(s_low, high[...], preferred_element_type=F32)
        kept = kept + jnp.dot(s_high, low[...], preferred_element_type=F32)
        kept = s.reshape(LEV, tall, length) - nudge_ref[on][:, :, None] * kept.reshape(LEV, tall, length)
        base[:, on, :] = jnp.swapaxes(kept, 0, 1)

    @pl.when(lat == 0)
    def _():
        recv[...] = jnp.zeros_like(recv)

    @pl.when(has_prev)
    def _():
        row_a.wait_recv()

    corner_copy.start()

    @pl.when(has_prev)
    def _():
        row_b.wait_recv()

    corner_copy.wait()
    project(recv, corner, x_top, qkv, top_at)
    key = lax.broadcasted_iota(jnp.int32, (1, 2 * half * WIN), 1)
    bias = jnp.where((key < half * WIN) & (lat == 0), -1e30, 0.0).astype(F32)
    attend(qkv, 2 * half * WIN, bias)

    top_copies = [remote(5 + j, send_top, d, prev, 1) for j, d in enumerate((d0, d1))]
    side_high = is_low & (lat == n_lat - 1)

    decode(top_at, x_top, [(None, send_top)])
    for j in range(2):

        @pl.when(has_prev & (lon == j))
        def _():
            top_copies[j].start()

    @pl.when(side_high)
    def _():
        to_high_last = remote(7, send_side, d0, lat, 1)
        to_high_last.start()

    decode(own_at, x_own, [(is_high, send_side), (is_low, d0)])

    @pl.when(is_high)
    def _():
        to_low_now = remote(8, send_side, d1, lat, 0)
        to_low_now.start()

    @pl.when(is_low)
    def _():
        remote(8, send_side, d1, lat, peer).wait_recv()

    @pl.when(is_high & has_next)
    def _():
        remote(5, send_top, d0, prev, 1).wait_recv()
        remote(6, send_top, d1, prev, 1).wait_recv()

    @pl.when(is_high & (lat == n_lat - 1))
    def _():
        remote(7, send_side, d0, lat, peer).wait_recv()

    part = PATCH * channels

    def nudge_rows(r):
        pieces = []
        for b in range(PATCH):
            for d in (d0, d1):
                pieces.append(d[b * part : (b + 1) * part, r * cols : (r + 1) * cols])
        x = jnp.concatenate(pieces, axis=1)
        kept = jnp.dot(x, dhigh[...], preferred_element_type=F32)
        kept = kept + jnp.dot(x, dlow[...], preferred_element_type=F32)
        y = r * PATCH
        base[y : y + PATCH] = base[y : y + PATCH] + nudge_ref[...][None] * kept.reshape(PATCH, channels, length)

    up_lat, up_lon = jnp.where(is_low, lat, nxt), peer
    down_lat, down_lon = jnp.where(is_low, prev, lat), peer
    inside_up, inside_down = is_low | has_next, is_high | has_prev
    up_copy = remote(9, up_rows, before, up_lat, up_lon)
    down_copy = remote(10, down_rows, after, down_lat, down_lon)
    count = tall // PATCH
    nudge_rows(count - 1)
    up_rows[...] = base[tall - 2 : tall].astype(BF16)

    @pl.when(inside_up)
    def _():
        up_copy.start()

    nudge_rows(0)
    down_rows[...] = base[0:2].astype(BF16)

    @pl.when(inside_down)
    def _():
        down_copy.start()

    for r in range(1, count - 1):
        nudge_rows(r)

    def row(y):
        if y < 0:
            return before[y + 2].astype(F32)
        if y >= tall:
            return after[y - tall].astype(F32)
        return base[y]

    def section(y):
        first[y + 1] = row(y) + time_step * tendency_row(row(y - 1), row(y), row(y + 1))

    @pl.loop(1, tall - 1)
    def _(y):
        first[y + 1] = base[y] + time_step * tendency_row(base[y - 1], base[y], base[y + 1])

    @pl.when(inside_down)
    def _():
        up_copy.wait_recv()

    @pl.when(jnp.logical_not(inside_down))
    def _():
        before[...] = jnp.zeros_like(before)

    @pl.when(inside_up)
    def _():
        down_copy.wait_recv()

    @pl.when(jnp.logical_not(inside_up))
    def _():
        after[...] = jnp.zeros_like(after)

    for y in (-1, 0, tall - 1, tall):
        section(y)
    first[0] = first[0] * jnp.where(inside_down, 1.0, 0.0)
    first[tall + 1] = first[tall + 1] * jnp.where(inside_up, 1.0, 0.0)

    @pl.loop(0, tall)
    def _(y):
        second = tendency_row(first[y], first[y + 1], first[y + 2])
        out_ref[y] = 0.5 * (base[y] + first[y + 1] + time_step * second)

    @pl.when(has_next)
    def _():
        row_a.wait_send()
        row_b.wait_send()

    for j in range(2):

        @pl.when(has_prev & (lon == j))
        def _():
            top_copies[j].wait_send()

    @pl.when(side_high)
    def _():
        remote(7, send_side, d0, lat, 1).wait_send()

    @pl.when(is_high)
    def _():
        remote(8, send_side, d1, lat, 0).wait_send()

    @pl.when(inside_up)
    def _():
        up_copy.wait_send()

    @pl.when(inside_down)
    def _():
        down_copy.wait_send()


def body(sizes, tokens, ln_gain, w_query, w_keyval, w_out, w_dec, nudge, state):
    half = WIN // 2
    cols, width = tokens.shape[1:]
    channels = nudge.shape[0]
    length = state.shape[2] * sizes["lon"]
    tall = state.shape[1] // sizes["lon"]
    windows = cols // WIN
    patches = w_dec.shape[1]
    strip = 16
    cells = half * WIN
    hbm, vmem = pl.BlockSpec(memory_space=pl.ANY), pl.BlockSpec(memory_space=pltpu.VMEM)
    V = pltpu.VMEM
    field = (tall, channels, length)
    flow = (patches, half * cols)
    scratch = [
        V((width, 3 * width), BF16), V((width, width), BF16), V(w_dec.shape, BF16), V((patches, width), BF16),
        V(tokens.shape, BF16), V((half, cols, width), BF16), V((2 * half, strip, width), BF16),
        V((half, strip, width), BF16),
        V((2, half, windows, WIN, width), F32), V((half, windows, WIN, width), F32),
        V((half, windows, WIN, width), F32),
        V((windows, 2 * cells, 3 * width), BF16), V((windows, cells, 3 * width), BF16),
        V((windows, 2 * cells, width), BF16), V((half * cols, width), BF16),
        V((channels, tall, length), F32), V(field, F32),
        V((length, length), BF16), V((length, length), BF16), V((length, length), BF16), V((length, length), BF16),
        V(flow, BF16), V(flow, BF16), V(flow, BF16), V(flow, BF16),
        V((2, channels, length), BF16), V((2, channels, length), BF16),
        V((2, channels, length), BF16), V((2, channels, length), BF16),
        V((tall + 2, channels, length), F32),
        pltpu.SemaphoreType.DMA((6,)), pltpu.SemaphoreType.DMA((11,)), pltpu.SemaphoreType.DMA((11,)),
    ]
    advanced = pl.pallas_call(
        functools.partial(cycle_kernel, sizes["lat"]),
        out_shape=jax.ShapeDtypeStruct(field, F32),
        in_specs=[hbm] * 6 + [vmem] * 4,
        out_specs=vmem,
        scratch_shapes=scratch,
        compiler_params=pltpu.CompilerParams(
            collective_id=0, has_side_effects=True, vmem_limit_bytes=62 * 2**20
        ),
        name="cycle",
    )(
        tokens, state, w_query, w_keyval, w_out, w_dec, ln_gain[None], nudge[:, None],
        jnp.asarray(filter_rows(length, KEEP, 1)), jnp.asarray(filter_rows(length, KEEP, PATCH)),
    )
    return advanced.transpose(1, 0, 2)


def tendency_row(south, centre, north):
    channels, length = centre.shape
    west = pltpu.roll(centre, 1, 1)
    east = pltpu.roll(centre, length - 1, 1)
    u = centre[:LEV][None]
    v = centre[LEV : 2 * LEV][None]
    dx = (east - west).reshape(VARS, LEV, length)
    dy = (north - south).reshape(VARS, LEV, length)
    advection = ((u * dx + v * dy) * 0.5).reshape(channels, length)
    return diffusion * (east + west + north + south - 4.0 * centre) - advection


def solution(mesh):
    in_specs = (
        P(("member", "lat"), "lon", None),
        P(),
        P(),
        P(),
        P(),
        P(),
        P(),
        P(None, ("member", "lat"), "lon"),
    )
    out_specs = P(None, ("member", "lat", "lon"), None)
    return jax.shard_map(
        functools.partial(body, dict(mesh.shape)),
        mesh=mesh,
        in_specs=in_specs,
        out_specs=out_specs,
        check_vma=False,
    )
```

```python
import functools
import math

import jax
import jax.numpy as jnp
import numpy as np
from jax import lax
from jax.experimental import pallas as pl
from jax.experimental.pallas import tpu as pltpu
from jax.sharding import PartitionSpec as P

HEADS = 16
WIN = 8
PATCH = 4
VARS = 4
LEV = 8
KEEP = 256

time_step = 0.1
diffusion = 0.5
epsilon = 1e-05
F32 = jnp.float32
BF16 = jnp.bfloat16
NT = (((1,), (1,)), ((), ()))


def filter_rows(length, kept, stride):
    offset = np.arange(length)
    waves = np.arange(1, kept)
    angles = 2.0 * np.pi * ((offset[:, None] * waves[None, :]) % length) / length
    kernel = (1.0 + 2.0 * np.cos(angles).sum(1)) / length
    return kernel[(offset[None, :] - stride * np.arange(16)[:, None]) % length].astype(np.float32)


def split(value):
    high = value.astype(BF16)
    return high, (value - high.astype(F32)).astype(BF16)


def cycle_kernel(
    n_lat, tokens, state, wq_hbm, wkv_hbm, wo_hbm, wd_hbm, gain_ref, nudge_ref, rows1_ref, rows4_ref, out_ref,
    wqkv, wo, wd, wdt, own, recv, edge, corner, xs, xs_b, normed, qkv, qkv_b, att, lo,
    band, base, high, low, dhigh, dlow, d0, d1, send_top, send_side, up_rows, down_rows, before, after, first,
    load_sem, send_sem, recv_sem,
):
    lat, lon = lax.axis_index("lat"), lax.axis_index("lon")
    half = WIN // 2
    cols, width = tokens.shape[1:]
    windows = cols // WIN
    strip = edge.shape[1]
    tall, channels, length = base.shape
    wide = state.shape[2]
    is_low, is_high = lon == 0, lon == 1
    has_prev, has_next = lat > 0, lat < n_lat - 1
    prev, nxt = jnp.maximum(lat - 1, 0), jnp.minimum(lat + 1, n_lat - 1)
    peer = 1 - lon

    def load(i, src, dst):
        return pltpu.make_async_copy(src, dst, load_sem.at[i])

    def remote(i, src, dst, to_lat, to_lon):
        return pltpu.make_async_remote_copy(
            src_ref=src, dst_ref=dst, send_sem=send_sem.at[i], recv_sem=recv_sem.at[i],
            device_id={"lat": to_lat, "lon": to_lon}, device_id_type=pl.DeviceIdType.MESH,
        )

    own_load = load(0, tokens, own)
    loads = [
        load(1, wq_hbm, wqkv.at[:, pl.ds(0, width)]),
        load(2, wkv_hbm, wqkv.at[:, pl.ds(width, 2 * width)]),
        load(3, wo_hbm, wo),
        load(4, wd_hbm, wd),
    ]
    my_rows = pl.ds(pl.multiple_of(lon * tall, 8), tall)
    peer_rows = pl.ds(pl.multiple_of(peer * tall, 8), tall)
    my_cols = pl.ds(pl.multiple_of(lon * wide, 128), wide)
    own_state = load(5, state.at[:, my_rows, :], band.at[:, :, my_cols])
    own_load.start()
    for item in loads:
        item.start()
    own_state.start()

    barrier = pltpu.get_barrier_semaphore()

    def greet(to_lat, to_lon):
        pl.semaphore_signal(
            barrier, inc=1, device_id={"lat": to_lat, "lon": to_lon}, device_id_type=pl.DeviceIdType.MESH
        )

    greet(lat, peer)

    @pl.when(has_prev)
    def _():
        greet(prev, lon)
        greet(prev, peer)

    @pl.when(has_next)
    def _():
        greet(nxt, lon)
        greet(nxt, peer)

    pl.semaphore_wait(barrier, 1 + 2 * has_prev.astype(jnp.int32) + 2 * has_next.astype(jnp.int32))

    row_a = remote(0, tokens.at[pl.ds(half, half), pl.ds(0, strip), :], recv.at[:, pl.ds(0, strip), :], nxt, lon)
    row_b = remote(
        1, tokens.at[pl.ds(half, half), pl.ds(strip, cols - strip), :],
        recv.at[:, pl.ds(strip, cols - strip), :], nxt, lon,
    )
    edge_copy = remote(2, tokens.at[:, pl.ds(0, strip), :], edge, lat, peer)
    state_copy = remote(3, state.at[:, peer_rows, :], band.at[:, :, my_cols], lat, peer)
    corner_copy = remote(4, recv.at[:, pl.ds(0, strip), :], corner, lat, peer)

    @pl.when(has_next)
    def _():
        row_a.start()
        row_b.start()

    edge_copy.start()
    state_copy.start()

    def project(block, strip_block, x_out, qkv_out, at):
        for r in range(half):
            row = block[r].astype(F32)
            side = strip_block[r].astype(F32)
            row = jnp.concatenate([row[half:], side[:half]], axis=0)
            centred = row - jnp.mean(row, axis=-1, keepdims=True)
            variance = jnp.mean(centred * centred, axis=-1, keepdims=True)
            unit = centred * lax.rsqrt(variance + epsilon) * gain_ref[...]
            x_out[r] = row.reshape(windows, WIN, width)
            normed[r] = unit.reshape(windows, WIN, width)
        flat = jnp.swapaxes(normed[...], 0, 1).reshape(windows * half * WIN, width).astype(BF16)
        scale = jnp.float32(1.0 / math.sqrt(width // HEADS))

        @pl.loop(0, 3 * width // 256)
        def _(n):
            on = pl.ds(pl.multiple_of(n * 256, 256), 256)
            value = jnp.dot(flat, wqkv[:, on], preferred_element_type=F32).astype(BF16)
            value = (value.astype(F32) * jnp.where(n < width // 256, scale, 1.0)).astype(BF16)
            qkv_out[:, at, on] = value.reshape(windows, half * WIN, 256)

    def attend(qkv_in, cells, bias):
        head = width // HEADS
        pair = 2 * head
        lanes = lax.broadcasted_iota(jnp.int32, (cells, pair), 1) < head

        @pl.loop(0, windows)
        def _(w):
            for group in range(0, HEADS // 2, 4):
                spots = [p * pair for p in range(group, group + 4)]
                scores = []
                for on in spots:
                    qp = qkv_in[w, :, on : on + pair]
                    zero = jnp.zeros_like(qp)
                    q2 = jnp.concatenate([jnp.where(lanes, qp, zero), jnp.where(lanes, zero, qp)], axis=0)
                    kp = qkv_in[w, :, width + on : width + on + pair]
                    s = lax.dot_general(q2, kp, NT, preferred_element_type=F32)
                    scores.append(s if bias is None else s + bias)
                peaks = [jnp.max(s, axis=-1, keepdims=True) for s in scores]
                powers = [jnp.exp(s - m).astype(BF16) for s, m in zip(scores, peaks)]
                mixed = []
                for on, e in zip(spots, powers):
                    vp = qkv_in[w, :, 2 * width + on : 2 * width + on + pair]
                    ones = jnp.ones_like(vp)
                    low_out = jnp.dot(e[:cells], jnp.where(lanes, vp, ones), preferred_element_type=F32)
                    high_out = jnp.dot(e[cells:], jnp.where(lanes, ones, vp), preferred_element_type=F32)
                    total = pltpu.roll(jnp.where(lanes, high_out, low_out), head, 1)
                    mixed.append((jnp.where(lanes, low_out, high_out) / total).astype(BF16))
                att[w, 0:cells, spots[0] : spots[0] + 4 * pair] = jnp.concatenate(mixed, axis=1)

    def decode(at, x_in, outs):
        mixed = att[:, at, :].reshape(windows * half * WIN, width)

        @pl.loop(0, width // 256)
        def _(n):
            on = pl.ds(pl.multiple_of(n * 256, 256), 256)
            update = jnp.dot(mixed, wo[:, on], preferred_element_type=F32)
            update = jnp.swapaxes(update.reshape(windows, half, WIN, 256), 0, 1)
            value = x_in[:, :, :, on] + update
            lo[:, on] = value.reshape(half * cols, 256).astype(BF16)

        value = lax.dot_general(wdt[...], lo[...], NT, preferred_element_type=F32).astype(BF16)
        for chosen_here, out in outs:
            if chosen_here is None:
                out[...] = value
            else:

                @pl.when(chosen_here)
                def _():
                    out[...] = value

    top_at, own_at = slice(0, half * WIN), slice(half * WIN, 2 * half * WIN)
    x_top, x_own = xs.at[0], xs.at[1]
    own_load.wait()
    edge_copy.wait()
    loads[0].wait()
    loads[1].wait()
    project(own.at[pl.ds(0, half)], edge.at[pl.ds(0, half)], x_own, qkv, own_at)

    loads[2].wait()
    loads[3].wait()
    patches = wdt.shape[0]
    row_id = lax.broadcasted_iota(jnp.int32, (patches, patches), 0)
    col_id = lax.broadcasted_iota(jnp.int32, (patches, patches), 1)
    area = PATCH * PATCH
    wanted = (row_id % channels) * area + (row_id // channels) % PATCH * PATCH + row_id // (PATCH * channels)
    chosen = (col_id == wanted).astype(F32).astype(BF16)
    wdt[...] = lax.dot_general(chosen, wd[...], NT, preferred_element_type=F32).astype(BF16)

    blocks = length // 16

    @pl.loop(0, blocks)
    def _(g):
        on = pl.ds(pl.multiple_of(g * 16, 16), 16)
        high[on, :], low[on, :] = split(pltpu.roll(rows1_ref[...], g * 16, 1))
        per = blocks // PATCH
        shift = lax.rem((lax.rem(g, per) * 16 + half) * PATCH + g // per, length)
        dhigh[on, :], dlow[on, :] = split(pltpu.roll(rows4_ref[...], shift, 1))

    own_state.wait()
    state_copy.wait()

    @pl.loop(0, channels // LEV)
    def _(g):
        on = pl.ds(pl.multiple_of(g * LEV, LEV), LEV)
        s = band[on].reshape(LEV * tall, length)
        s_high, s_low = split(s)
        kept = jnp.dot(s_high, high[...], preferred_element_type=F32)
        kept = kept + jnp.dot(s_low, high[...], preferred_element_type=F32)
        kept = kept + jnp.dot(s_high, low[...], preferred_element_type=F32)
        kept = s.reshape(LEV, tall, length) - nudge_ref[on][:, :, None] * kept.reshape(LEV, tall, length)
        base[:, on, :] = jnp.swapaxes(kept, 0, 1)

    @pl.when(lat == 0)
    def _():
        recv[...] = jnp.zeros_like(recv)

    @pl.when(has_prev)
    def _():
        row_a.wait_recv()

    corner_copy.start()

    @pl.when(has_prev)
    def _():
        row_b.wait_recv()

    corner_copy.wait()
    project(recv, corner, x_top, qkv, top_at)
    key = lax.broadcasted_iota(jnp.int32, (1, 2 * half * WIN), 1)
    bias = jnp.where((key < half * WIN) & (lat == 0), -1e30, 0.0).astype(F32)
    attend(qkv, 2 * half * WIN, bias)

    top_copies = [remote(5 + j, send_top, d, prev, 1) for j, d in enumerate((d0, d1))]
    side_high = is_low & (lat == n_lat - 1)

    decode(top_at, x_top, [(None, send_top)])
    for j in range(2):

        @pl.when(has_prev & (lon == j))
        def _():
            top_copies[j].start()

    decode(own_at, x_own, [(is_high, send_side), (is_low, d0)])

    @pl.when(is_high)
    def _():
        to_low_now = remote(8, send_side, d1, lat, 0)
        to_low_now.start()

    @pl.when(lat == n_lat - 1)
    def _():
        project(own.at[pl.ds(half, half)], edge.at[pl.ds(half, half)], xs_b, qkv_b, top_at)
        attend(qkv_b, half * WIN, None)
        decode(top_at, xs_b, [(is_high, d1), (is_low, send_side)])

    @pl.when(side_high)
    def _():
        to_high_last = remote(7, send_side, d0, lat, 1)
        to_high_last.start()

    @pl.when(is_low)
    def _():
        remote(8, send_side, d1, lat, peer).wait_recv()

    @pl.when(is_high & has_next)
    def _():
        remote(5, send_top, d0, prev, 1).wait_recv()
        remote(6, send_top, d1, prev, 1).wait_recv()

    @pl.when(is_high & (lat == n_lat - 1))
    def _():
        remote(7, send_side, d0, lat, peer).wait_recv()

    part = PATCH * channels

    def nudge_rows(r):
        pieces = []
        for b in range(PATCH):
            for d in (d0, d1):
                pieces.append(d[b * part : (b + 1) * part, r * cols : (r + 1) * cols])
        x = jnp.concatenate(pieces, axis=1)
        kept = jnp.dot(x, dhigh[...], preferred_element_type=F32)
        kept = kept + jnp.dot(x, dlow[...], preferred_element_type=F32)
        y = r * PATCH
        base[y : y + PATCH] = base[y : y + PATCH] + nudge_ref[...][None] * kept.reshape(PATCH, channels, length)

    up_lat, up_lon = jnp.where(is_low, lat, nxt), peer
    down_lat, down_lon = jnp.where(is_low, prev, lat), peer
    inside_up, inside_down = is_low | has_next, is_high | has_prev
    up_copy = remote(9, up_rows, before, up_lat, up_lon)
    down_copy = remote(10, down_rows, after, down_lat, down_lon)
    count = tall // PATCH
    nudge_rows(count - 1)
    up_rows[...] = base[tall - 2 : tall].astype(BF16)

    @pl.when(inside_up)
    def _():
        up_copy.start()

    nudge_rows(0)
    down_rows[...] = base[0:2].astype(BF16)

    @pl.when(inside_down)
    def _():
        down_copy.start()

    for r in range(1, count - 1):
        nudge_rows(r)

    def row(y):
        if y < 0:
            return before[y + 2].astype(F32)
        if y >= tall:
            return after[y - tall].astype(F32)
        return base[y]

    def section(y):
        first[y + 1] = row(y) + time_step * tendency_row(row(y - 1), row(y), row(y + 1))

    @pl.loop(1, tall - 1)
    def _(y):
        first[y + 1] = base[y] + time_step * tendency_row(base[y - 1], base[y], base[y + 1])

    @pl.when(inside_down)
    def _():
        up_copy.wait_recv()

    @pl.when(jnp.logical_not(inside_down))
    def _():
        before[...] = jnp.zeros_like(before)

    @pl.when(inside_up)
    def _():
        down_copy.wait_recv()

    @pl.when(jnp.logical_not(inside_up))
    def _():
        after[...] = jnp.zeros_like(after)

    for y in (-1, 0, tall - 1, tall):
        section(y)
    first[0] = first[0] * jnp.where(inside_down, 1.0, 0.0)
    first[tall + 1] = first[tall + 1] * jnp.where(inside_up, 1.0, 0.0)

    @pl.loop(0, tall)
    def _(y):
        second = tendency_row(first[y], first[y + 1], first[y + 2])
        out_ref[y] = 0.5 * (base[y] + first[y + 1] + time_step * second)

    @pl.when(has_next)
    def _():
        row_a.wait_send()
        row_b.wait_send()

    for j in range(2):

        @pl.when(has_prev & (lon == j))
        def _():
            top_copies[j].wait_send()

    @pl.when(side_high)
    def _():
        remote(7, send_side, d0, lat, 1).wait_send()

    @pl.when(is_high)
    def _():
        remote(8, send_side, d1, lat, 0).wait_send()

    @pl.when(inside_up)
    def _():
        up_copy.wait_send()

    @pl.when(inside_down)
    def _():
        down_copy.wait_send()


def body(sizes, tokens, ln_gain, w_query, w_keyval, w_out, w_dec, nudge, state):
    half = WIN // 2
    cols, width = tokens.shape[1:]
    channels = nudge.shape[0]
    length = state.shape[2] * sizes["lon"]
    tall = state.shape[1] // sizes["lon"]
    windows = cols // WIN
    patches = w_dec.shape[1]
    strip = 16
    cells = half * WIN
    hbm, vmem = pl.BlockSpec(memory_space=pl.ANY), pl.BlockSpec(memory_space=pltpu.VMEM)
    V = pltpu.VMEM
    field = (tall, channels, length)
    flow = (patches, half * cols)
    scratch = [
        V((width, 3 * width), BF16), V((width, width), BF16), V(w_dec.shape, BF16), V((patches, width), BF16),
        V(tokens.shape, BF16), V((half, cols, width), BF16), V((2 * half, strip, width), BF16),
        V((half, strip, width), BF16),
        V((2, half, windows, WIN, width), F32), V((half, windows, WIN, width), F32),
        V((half, windows, WIN, width), F32),
        V((windows, 2 * cells, 3 * width), BF16), V((windows, cells, 3 * width), BF16),
        V((windows, 2 * cells, width), BF16), V((half * cols, width), BF16),
        V((channels, tall, length), F32), V(field, F32),
        V((length, length), BF16), V((length, length), BF16), V((length, length), BF16), V((length, length), BF16),
        V(flow, BF16), V(flow, BF16), V(flow, BF16), V(flow, BF16),
        V((2, channels, length), BF16), V((2, channels, length), BF16),
        V((2, channels, length), BF16), V((2, channels, length), BF16),
        V((tall + 2, channels, length), F32),
        pltpu.SemaphoreType.DMA((6,)), pltpu.SemaphoreType.DMA((11,)), pltpu.SemaphoreType.DMA((11,)),
    ]
    advanced = pl.pallas_call(
        functools.partial(cycle_kernel, sizes["lat"]),
        out_shape=jax.ShapeDtypeStruct(field, F32),
        in_specs=[hbm] * 6 + [vmem] * 4,
        out_specs=vmem,
        scratch_shapes=scratch,
        compiler_params=pltpu.CompilerParams(
            collective_id=0, has_side_effects=True, vmem_limit_bytes=62 * 2**20
        ),
        name="cycle",
    )(
        tokens, state, w_query, w_keyval, w_out, w_dec, ln_gain[None], nudge[:, None],
        jnp.asarray(filter_rows(length, KEEP, 1)), jnp.asarray(filter_rows(length, KEEP, PATCH)),
    )
    return advanced.transpose(1, 0, 2)


def tendency_row(south, centre, north):
    channels, length = centre.shape
    west = pltpu.roll(centre, 1, 1)
    east = pltpu.roll(centre, length - 1, 1)
    u = centre[:LEV][None]
    v = centre[LEV : 2 * LEV][None]
    dx = (east - west).reshape(VARS, LEV, length)
    dy = (north - south).reshape(VARS, LEV, length)
    advection = ((u * dx + v * dy) * 0.5).reshape(channels, length)
    return diffusion * (east + west + north + south - 4.0 * centre) - advection


def solution(mesh):
    in_specs = (
        P(("member", "lat"), "lon", None),
        P(),
        P(),
        P(),
        P(),
        P(),
        P(),
        P(None, ("member", "lat"), "lon"),
    )
    out_specs = P(None, ("member", "lat", "lon"), None)
    return jax.shard_map(
        functools.partial(body, dict(mesh.shape)),
        mesh=mesh,
        in_specs=in_specs,
        out_specs=out_specs,
        check_vma=False,
    )
```

```python
import functools
import math

import jax
import jax.numpy as jnp
import ml_dtypes
import numpy as np
from jax import lax
from jax.experimental import pallas as pl
from jax.experimental.pallas import tpu as pltpu
from jax.sharding import PartitionSpec as P

HEADS = 16
WIN = 8
PATCH = 4
VARS = 4
LEV = 8
KEEP = 256

time_step = 0.1
diffusion = 0.5
epsilon = 1e-05
F32 = jnp.float32
BF16 = jnp.bfloat16
NT = (((1,), (1,)), ((), ()))


def filter_rows(length, kept, stride, first):
    offset = np.arange(length)
    waves = np.arange(1, kept)
    angles = 2.0 * np.pi * ((offset[:, None] * waves[None, :]) % length) / length
    kernel = (1.0 + 2.0 * np.cos(angles).sum(1)) / length
    moved = offset[None, None, :] - stride * np.arange(16)[None, :, None] - np.asarray(first)[:, None, None]
    rows = kernel[moved % length].astype(np.float32)
    high = rows.astype(ml_dtypes.bfloat16)
    return jnp.asarray(np.stack([high, (rows - high.astype(np.float32)).astype(ml_dtypes.bfloat16)]))


def block_starts(length):
    blocks = length // 16
    per = blocks // PATCH
    plain = [16 * g for g in range(blocks)]
    patch = [((g % per * 16 + WIN // 2) * PATCH + g // per) % length for g in range(blocks)]
    return plain, patch


def split(value):
    high = value.astype(BF16)
    return high, (value - high.astype(F32)).astype(BF16)


def cycle_kernel(
    n_lat, tokens, state, wq_hbm, wkv_hbm, wo_hbm, wd_hbm, gain_ref, nudge_ref, rows1_ref, rows4_ref, out_ref,
    wqkv, wo, wd, wdt, own, recv, edge, corner, xs, xs_b, normed, qkv, qkv_b, att, lo,
    band, base, high, low, dhigh, dlow, d0, d1, send_top, send_side, up_rows, down_rows, before, after, first, strength,
    load_sem, send_sem, recv_sem,
):
    lat, lon = lax.axis_index("lat"), lax.axis_index("lon")
    half = WIN // 2
    cols, width = tokens.shape[1:]
    windows = cols // WIN
    strip = edge.shape[1]
    tall, channels, length = base.shape
    wide = state.shape[2]
    is_low, is_high = lon == 0, lon == 1
    has_prev, has_next = lat > 0, lat < n_lat - 1
    prev, nxt = jnp.maximum(lat - 1, 0), jnp.minimum(lat + 1, n_lat - 1)
    peer = 1 - lon

    def load(i, src, dst):
        return pltpu.make_async_copy(src, dst, load_sem.at[i])

    def remote(i, src, dst, to_lat, to_lon):
        return pltpu.make_async_remote_copy(
            src_ref=src, dst_ref=dst, send_sem=send_sem.at[i], recv_sem=recv_sem.at[i],
            device_id={"lat": to_lat, "lon": to_lon}, device_id_type=pl.DeviceIdType.MESH,
        )

    own_load = load(0, tokens, own)
    loads = [
        load(1, wq_hbm, wqkv.at[:, pl.ds(0, width)]),
        load(2, wkv_hbm, wqkv.at[:, pl.ds(width, 2 * width)]),
        load(3, wo_hbm, wo),
        load(4, wd_hbm, wd),
    ]
    my_rows = pl.ds(pl.multiple_of(lon * tall, 8), tall)
    peer_rows = pl.ds(pl.multiple_of(peer * tall, 8), tall)
    my_cols = pl.ds(pl.multiple_of(lon * wide, 128), wide)
    own_state = load(5, state.at[:, my_rows, :], band.at[:, :, my_cols])
    own_load.start()
    for item in loads:
        item.start()
    own_state.start()

    barrier = pltpu.get_barrier_semaphore()

    def greet(to_lat, to_lon):
        pl.semaphore_signal(
            barrier, inc=1, device_id={"lat": to_lat, "lon": to_lon}, device_id_type=pl.DeviceIdType.MESH
        )

    greet(lat, peer)

    @pl.when(has_prev)
    def _():
        greet(prev, lon)
        greet(prev, peer)

    @pl.when(has_next)
    def _():
        greet(nxt, lon)
        greet(nxt, peer)

    pl.semaphore_wait(barrier, 1 + 2 * has_prev.astype(jnp.int32) + 2 * has_next.astype(jnp.int32))

    row_a = remote(0, tokens.at[pl.ds(half, half), pl.ds(0, strip), :], recv.at[:, pl.ds(0, strip), :], nxt, lon)
    row_b = remote(
        1, tokens.at[pl.ds(half, half), pl.ds(strip, cols - strip), :],
        recv.at[:, pl.ds(strip, cols - strip), :], nxt, lon,
    )
    edge_copy = remote(2, tokens.at[:, pl.ds(0, strip), :], edge, lat, peer)
    state_copy = remote(3, state.at[:, peer_rows, :], band.at[:, :, my_cols], lat, peer)
    corner_copy = remote(4, recv.at[:, pl.ds(0, strip), :], corner, lat, peer)

    @pl.when(has_next)
    def _():
        row_a.start()
        row_b.start()

    edge_copy.start()
    state_copy.start()

    def project(block, strip_block, x_out, qkv_out, at):
        for r in range(half):
            row = block[r].astype(F32)
            side = strip_block[r].astype(F32)
            row = jnp.concatenate([row[half:], side[:half]], axis=0)
            centred = row - jnp.mean(row, axis=-1, keepdims=True)
            variance = jnp.mean(centred * centred, axis=-1, keepdims=True)
            unit = centred * lax.rsqrt(variance + epsilon) * gain_ref[...]
            x_out[r] = row.reshape(windows, WIN, width)
            normed[r] = unit.reshape(windows, WIN, width)
        flat = jnp.swapaxes(normed[...], 0, 1).reshape(windows * half * WIN, width).astype(BF16)
        scale = jnp.float32(1.0 / math.sqrt(width // HEADS))

        @pl.loop(0, 3 * width // 256)
        def _(n):
            on = pl.ds(pl.multiple_of(n * 256, 256), 256)
            value = jnp.dot(flat, wqkv[:, on], preferred_element_type=F32).astype(BF16)
            value = (value.astype(F32) * jnp.where(n < width // 256, scale, 1.0)).astype(BF16)
            qkv_out[:, at, on] = value.reshape(windows, half * WIN, 256)

    def attend(qkv_in, cells, bias):
        head = width // HEADS
        pair = 2 * head
        lanes = lax.broadcasted_iota(jnp.int32, (cells, pair), 1) < head

        @pl.loop(0, windows, unroll=2)
        def _(w):
            for group in range(0, HEADS // 2, 4):
                spots = [p * pair for p in range(group, group + 4)]
                scores = []
                for on in spots:
                    qp = qkv_in[w, :, on : on + pair]
                    zero = jnp.zeros_like(qp)
                    q2 = jnp.concatenate([jnp.where(lanes, qp, zero), jnp.where(lanes, zero, qp)], axis=0)
                    kp = qkv_in[w, :, width + on : width + on + pair]
                    s = lax.dot_general(q2, kp, NT, preferred_element_type=F32)
                    scores.append(s if bias is None else s + bias)
                peaks = [jnp.max(s, axis=-1, keepdims=True) for s in scores]
                powers = [jnp.exp(s - m).astype(BF16) for s, m in zip(scores, peaks)]
                mixed = []
                for on, e in zip(spots, powers):
                    vp = qkv_in[w, :, 2 * width + on : 2 * width + on + pair]
                    ones = jnp.ones_like(vp)
                    low_out = jnp.dot(e[:cells], jnp.where(lanes, vp, ones), preferred_element_type=F32)
                    high_out = jnp.dot(e[cells:], jnp.where(lanes, ones, vp), preferred_element_type=F32)
                    total = pltpu.roll(jnp.where(lanes, high_out, low_out), head, 1)
                    mixed.append((jnp.where(lanes, low_out, high_out) / total).astype(BF16))
                att[w, 0:cells, spots[0] : spots[0] + 4 * pair] = jnp.concatenate(mixed, axis=1)

    def decode(at, x_in, outs):
        mixed = att[:, at, :].reshape(windows * half * WIN, width)

        @pl.loop(0, width // 256)
        def _(n):
            on = pl.ds(pl.multiple_of(n * 256, 256), 256)
            update = jnp.dot(mixed, wo[:, on], preferred_element_type=F32)
            update = jnp.swapaxes(update.reshape(windows, half, WIN, 256), 0, 1)
            value = x_in[:, :, :, on] + update
            lo[:, on] = value.reshape(half * cols, 256).astype(BF16)

        value = lax.dot_general(wdt[...], lo[...], NT, preferred_element_type=F32).astype(BF16)
        for chosen_here, out in outs:
            if chosen_here is None:
                out[...] = value
            else:

                @pl.when(chosen_here)
                def _():
                    out[...] = value

    top_at, own_at = slice(0, half * WIN), slice(half * WIN, 2 * half * WIN)
    x_top, x_own = xs.at[0], xs.at[1]
    own_load.wait()
    edge_copy.wait()
    loads[0].wait()
    loads[1].wait()
    project(own.at[pl.ds(0, half)], edge.at[pl.ds(0, half)], x_own, qkv, own_at)

    loads[2].wait()
    loads[3].wait()
    patches = wdt.shape[0]
    row_id = lax.broadcasted_iota(jnp.int32, (patches, patches), 0)
    col_id = lax.broadcasted_iota(jnp.int32, (patches, patches), 1)
    area = PATCH * PATCH
    wanted = (row_id % channels) * area + (row_id // channels) % PATCH * PATCH + row_id // (PATCH * channels)
    chosen = (col_id == wanted).astype(F32).astype(BF16)
    wdt[...] = lax.dot_general(chosen, wd[...], NT, preferred_element_type=F32).astype(BF16)

    @pl.when(lat == n_lat - 1)
    def _():
        project(own.at[pl.ds(half, half)], edge.at[pl.ds(half, half)], xs_b, qkv_b, top_at)

    for starts, source, tables in zip(block_starts(length), (rows1_ref, rows4_ref), ((high, low), (dhigh, dlow))):
        bases = sorted({start % 128 for start in starts})
        for g, start in enumerate(starts):
            cut = length - start // 128 * 128
            for j in range(2):
                value = source[j, bases.index(start % 128)]
                if cut < length:
                    value = jnp.concatenate([value[:, cut:], value[:, :cut]], axis=1)
                tables[j][16 * g : 16 * g + 16, :] = value

    eye = lax.broadcasted_iota(jnp.int32, (channels, channels), 0)
    eye = eye == lax.broadcasted_iota(jnp.int32, (channels, channels), 1)
    strength[...] = jnp.sum(jnp.where(eye, nudge_ref[...], 0.0), axis=1, keepdims=True)

    own_state.wait()
    state_copy.wait()

    @pl.loop(0, channels // LEV)
    def _(g):
        on = pl.ds(pl.multiple_of(g * LEV, LEV), LEV)
        s = band[on].reshape(LEV * tall, length)
        s_high, s_low = split(s)
        kept = jnp.dot(s_high, high[...], preferred_element_type=F32)
        kept = kept + jnp.dot(s_low, high[...], preferred_element_type=F32)
        kept = kept + jnp.dot(s_high, low[...], preferred_element_type=F32)
        kept = s.reshape(LEV, tall, length) - strength[on][:, :, None] * kept.reshape(LEV, tall, length)
        base[:, on, :] = jnp.swapaxes(kept, 0, 1)

    @pl.when(lat == 0)
    def _():
        recv[...] = jnp.zeros_like(recv)

    @pl.when(has_prev)
    def _():
        row_a.wait_recv()

    corner_copy.start()

    @pl.when(has_prev)
    def _():
        row_b.wait_recv()

    corner_copy.wait()
    project(recv, corner, x_top, qkv, top_at)
    key = lax.broadcasted_iota(jnp.int32, (1, 2 * half * WIN), 1)
    bias = jnp.where((key < half * WIN) & (lat == 0), -1e30, 0.0).astype(F32)
    attend(qkv, 2 * half * WIN, bias)

    top_copies = [remote(5 + j, send_top, d, prev, 1) for j, d in enumerate((d0, d1))]
    side_high = is_low & (lat == n_lat - 1)

    decode(top_at, x_top, [(None, send_top)])
    for j in range(2):

        @pl.when(has_prev & (lon == j))
        def _():
            top_copies[j].start()

    decode(own_at, x_own, [(is_high, send_side), (is_low, d0)])

    @pl.when(is_high)
    def _():
        to_low_now = remote(8, send_side, d1, lat, 0)
        to_low_now.start()

    @pl.when(lat == n_lat - 1)
    def _():
        attend(qkv_b, half * WIN, None)
        decode(top_at, xs_b, [(is_high, d1), (is_low, send_side)])

    @pl.when(side_high)
    def _():
        to_high_last = remote(7, send_side, d0, lat, 1)
        to_high_last.start()

    @pl.when(is_low)
    def _():
        remote(8, send_side, d1, lat, peer).wait_recv()

    @pl.when(is_high & has_next)
    def _():
        remote(5, send_top, d0, prev, 1).wait_recv()
        remote(6, send_top, d1, prev, 1).wait_recv()

    @pl.when(is_high & (lat == n_lat - 1))
    def _():
        remote(7, send_side, d0, lat, peer).wait_recv()

    part = PATCH * channels

    def nudge_rows(r):
        pieces = []
        for b in range(PATCH):
            for d in (d0, d1):
                pieces.append(d[b * part : (b + 1) * part, r * cols : (r + 1) * cols])
        x = jnp.concatenate(pieces, axis=1)
        kept = jnp.dot(x, dhigh[...], preferred_element_type=F32)
        kept = kept + jnp.dot(x, dlow[...], preferred_element_type=F32)
        y = r * PATCH
        base[y : y + PATCH] = base[y : y + PATCH] + strength[...][None] * kept.reshape(PATCH, channels, length)

    up_lat, up_lon = jnp.where(is_low, lat, nxt), peer
    down_lat, down_lon = jnp.where(is_low, prev, lat), peer
    inside_up, inside_down = is_low | has_next, is_high | has_prev
    up_copy = remote(9, up_rows, before, up_lat, up_lon)
    down_copy = remote(10, down_rows, after, down_lat, down_lon)
    count = tall // PATCH
    nudge_rows(count - 1)
    up_rows[...] = base[tall - 2 : tall].astype(BF16)

    @pl.when(inside_up)
    def _():
        up_copy.start()

    nudge_rows(0)
    down_rows[...] = base[0:2].astype(BF16)

    @pl.when(inside_down)
    def _():
        down_copy.start()

    for r in range(1, count - 1):
        nudge_rows(r)

    def row(y):
        if y < 0:
            return before[y + 2].astype(F32)
        if y >= tall:
            return after[y - tall].astype(F32)
        return base[y]

    def section(y):
        first[y + 1] = row(y) + time_step * tendency_row(row(y - 1), row(y), row(y + 1))

    @pl.loop(1, tall - 1)
    def _(y):
        first[y + 1] = base[y] + time_step * tendency_row(base[y - 1], base[y], base[y + 1])

    @pl.when(inside_down)
    def _():
        up_copy.wait_recv()

    @pl.when(jnp.logical_not(inside_down))
    def _():
        before[...] = jnp.zeros_like(before)

    @pl.when(inside_up)
    def _():
        down_copy.wait_recv()

    @pl.when(jnp.logical_not(inside_up))
    def _():
        after[...] = jnp.zeros_like(after)

    for y in (-1, 0, tall - 1, tall):
        section(y)
    first[0] = first[0] * jnp.where(inside_down, 1.0, 0.0)
    first[tall + 1] = first[tall + 1] * jnp.where(inside_up, 1.0, 0.0)

    @pl.loop(0, tall)
    def _(y):
        second = tendency_row(first[y], first[y + 1], first[y + 2])
        out_ref[y] = 0.5 * (base[y] + first[y + 1] + time_step * second)

    @pl.when(has_next)
    def _():
        row_a.wait_send()
        row_b.wait_send()

    for j in range(2):

        @pl.when(has_prev & (lon == j))
        def _():
            top_copies[j].wait_send()

    @pl.when(side_high)
    def _():
        remote(7, send_side, d0, lat, 1).wait_send()

    @pl.when(is_high)
    def _():
        remote(8, send_side, d1, lat, 0).wait_send()

    @pl.when(inside_up)
    def _():
        up_copy.wait_send()

    @pl.when(inside_down)
    def _():
        down_copy.wait_send()


def body(sizes, tokens, ln_gain, w_query, w_keyval, w_out, w_dec, nudge, state):
    half = WIN // 2
    cols, width = tokens.shape[1:]
    channels = nudge.shape[0]
    length = state.shape[2] * sizes["lon"]
    tall = state.shape[1] // sizes["lon"]
    windows = cols // WIN
    patches = w_dec.shape[1]
    strip = 16
    cells = half * WIN
    hbm, vmem = pl.BlockSpec(memory_space=pl.ANY), pl.BlockSpec(memory_space=pltpu.VMEM)
    V = pltpu.VMEM
    field = (tall, channels, length)
    flow = (patches, half * cols)
    scratch = [
        V((width, 3 * width), BF16), V((width, width), BF16), V(w_dec.shape, BF16), V((patches, width), BF16),
        V(tokens.shape, BF16), V((half, cols, width), BF16), V((2 * half, strip, width), BF16),
        V((half, strip, width), BF16),
        V((2, half, windows, WIN, width), F32), V((half, windows, WIN, width), F32),
        V((half, windows, WIN, width), F32),
        V((windows, 2 * cells, 3 * width), BF16), V((windows, cells, 3 * width), BF16),
        V((windows, 2 * cells, width), BF16), V((half * cols, width), BF16),
        V((channels, tall, length), F32), V(field, F32),
        V((length, length), BF16), V((length, length), BF16), V((length, length), BF16), V((length, length), BF16),
        V(flow, BF16), V(flow, BF16), V(flow, BF16), V(flow, BF16),
        V((2, channels, length), BF16), V((2, channels, length), BF16),
        V((2, channels, length), BF16), V((2, channels, length), BF16),
        V((tall + 2, channels, length), F32), V((channels, 1), F32),
        pltpu.SemaphoreType.DMA((6,)), pltpu.SemaphoreType.DMA((11,)), pltpu.SemaphoreType.DMA((11,)),
    ]
    tables = [
        filter_rows(length, KEEP, stride, sorted({start % 128 for start in starts}))
        for stride, starts in zip((1, PATCH), block_starts(length))
    ]
    advanced = pl.pallas_call(
        functools.partial(cycle_kernel, sizes["lat"]),
        out_shape=jax.ShapeDtypeStruct(field, F32),
        in_specs=[hbm] * 6 + [vmem] * 4,
        out_specs=vmem,
        scratch_shapes=scratch,
        compiler_params=pltpu.CompilerParams(
            collective_id=0, has_side_effects=True, vmem_limit_bytes=62 * 2**20
        ),
        name="cycle",
    )(
        tokens, state, w_query, w_keyval, w_out, w_dec, ln_gain[None], nudge[None],
        *tables,
    )
    return advanced.transpose(1, 0, 2)


def tendency_row(south, centre, north):
    channels, length = centre.shape
    west = pltpu.roll(centre, 1, 1)
    east = pltpu.roll(centre, length - 1, 1)
    u = centre[:LEV][None]
    v = centre[LEV : 2 * LEV][None]
    dx = (east - west).reshape(VARS, LEV, length)
    dy = (north - south).reshape(VARS, LEV, length)
    advection = ((u * dx + v * dy) * 0.5).reshape(channels, length)
    return diffusion * (east + west + north + south - 4.0 * centre) - advection


def solution(mesh):
    in_specs = (
        P(("member", "lat"), "lon", None),
        P(),
        P(),
        P(),
        P(),
        P(),
        P(),
        P(None, ("member", "lat"), "lon"),
    )
    out_specs = P(None, ("member", "lat", "lon"), None)
    return jax.shard_map(
        functools.partial(body, dict(mesh.shape)),
        mesh=mesh,
        in_specs=in_specs,
        out_specs=out_specs,
        check_vma=False,
    )
```

```python
import functools
import math

import jax
import jax.numpy as jnp
import ml_dtypes
import numpy as np
from jax import lax
from jax.experimental import pallas as pl
from jax.experimental.pallas import tpu as pltpu
from jax.sharding import PartitionSpec as P

HEADS = 16
WIN = 8
PATCH = 4
VARS = 4
LEV = 8
KEEP = 256

time_step = 0.1
diffusion = 0.5
epsilon = 1e-05
F32 = jnp.float32
BF16 = jnp.bfloat16
NT = (((1,), (1,)), ((), ()))


def filter_rows(length, kept, stride, first):
    offset = np.arange(length)
    waves = np.arange(1, kept)
    angles = 2.0 * np.pi * ((offset[:, None] * waves[None, :]) % length) / length
    kernel = (1.0 + 2.0 * np.cos(angles).sum(1)) / length
    moved = offset[None, None, :] - stride * np.arange(16)[None, :, None] - np.asarray(first)[:, None, None]
    rows = kernel[moved % length].astype(np.float32)
    high = rows.astype(ml_dtypes.bfloat16)
    return jnp.asarray(np.stack([high, (rows - high.astype(np.float32)).astype(ml_dtypes.bfloat16)]))


def block_starts(length):
    blocks = length // 16
    per = blocks // PATCH
    plain = [16 * g for g in range(blocks)]
    patch = [((g % per * 16 + WIN // 2) * PATCH + g // per) % length for g in range(blocks)]
    return plain, patch


def split(value):
    high = value.astype(BF16)
    return high, (value - high.astype(F32)).astype(BF16)


def cycle_kernel(
    n_lat, tokens, state, wq_hbm, wkv_hbm, wo_hbm, wd_hbm, gain_ref, nudge_ref, rows1_ref, rows4_ref, out_ref,
    wqkv, wo, wd, wdt, own, recv, edge, corner, xs, xs_b, normed, qkv, qkv_b, att, lo,
    band, base, high, low, dhigh, dlow, d0, d1, send_top, send_side, up_rows, down_rows, before, after, first, strength,
    load_sem, send_sem, recv_sem,
):
    lat, lon = lax.axis_index("lat"), lax.axis_index("lon")
    half = WIN // 2
    cols, width = tokens.shape[1:]
    windows = cols // WIN
    strip = edge.shape[1]
    tall, channels, length = base.shape
    wide = state.shape[2]
    is_low, is_high = lon == 0, lon == 1
    has_prev, has_next = lat > 0, lat < n_lat - 1
    prev, nxt = jnp.maximum(lat - 1, 0), jnp.minimum(lat + 1, n_lat - 1)
    peer = 1 - lon

    def load(i, src, dst):
        return pltpu.make_async_copy(src, dst, load_sem.at[i])

    def remote(i, src, dst, to_lat, to_lon):
        return pltpu.make_async_remote_copy(
            src_ref=src, dst_ref=dst, send_sem=send_sem.at[i], recv_sem=recv_sem.at[i],
            device_id={"lat": to_lat, "lon": to_lon}, device_id_type=pl.DeviceIdType.MESH,
        )

    own_load = load(0, tokens, own)
    loads = [
        load(1, wq_hbm, wqkv.at[:, pl.ds(0, width)]),
        load(2, wkv_hbm, wqkv.at[:, pl.ds(width, 2 * width)]),
        load(3, wo_hbm, wo),
        load(4, wd_hbm, wd),
    ]
    my_rows = pl.ds(pl.multiple_of(lon * tall, 8), tall)
    peer_rows = pl.ds(pl.multiple_of(peer * tall, 8), tall)
    my_cols = pl.ds(pl.multiple_of(lon * wide, 128), wide)
    own_state = load(5, state.at[:, my_rows, :], band.at[:, :, my_cols])
    own_load.start()
    for item in loads:
        item.start()
    own_state.start()

    barrier = pltpu.get_barrier_semaphore()

    def greet(to_lat, to_lon):
        pl.semaphore_signal(
            barrier, inc=1, device_id={"lat": to_lat, "lon": to_lon}, device_id_type=pl.DeviceIdType.MESH
        )

    greet(lat, peer)

    @pl.when(has_prev)
    def _():
        greet(prev, lon)
        greet(prev, peer)

    @pl.when(has_next)
    def _():
        greet(nxt, lon)
        greet(nxt, peer)

    pl.semaphore_wait(barrier, 1 + 2 * has_prev.astype(jnp.int32) + 2 * has_next.astype(jnp.int32))

    row_a = remote(0, tokens.at[pl.ds(half, half), pl.ds(0, strip), :], recv.at[:, pl.ds(0, strip), :], nxt, lon)
    row_b = remote(
        1, tokens.at[pl.ds(half, half), pl.ds(strip, cols - strip), :],
        recv.at[:, pl.ds(strip, cols - strip), :], nxt, lon,
    )
    edge_copy = remote(2, tokens.at[:, pl.ds(0, strip), :], edge, lat, peer)
    state_copy = remote(3, state.at[:, peer_rows, :], band.at[:, :, my_cols], lat, peer)
    corner_copy = remote(4, recv.at[:, pl.ds(0, strip), :], corner, lat, peer)

    @pl.when(has_next)
    def _():
        row_a.start()
        row_b.start()

    edge_copy.start()
    state_copy.start()

    def project(block, strip_block, x_out, qkv_out, at):
        for r in range(half):
            row = block[r].astype(F32)
            side = strip_block[r].astype(F32)
            row = jnp.concatenate([row[half:], side[:half]], axis=0)
            centred = row - jnp.mean(row, axis=-1, keepdims=True)
            variance = jnp.mean(centred * centred, axis=-1, keepdims=True)
            unit = centred * lax.rsqrt(variance + epsilon) * gain_ref[...]
            x_out[r] = row.reshape(windows, WIN, width)
            normed[r] = unit.reshape(windows, WIN, width)
        flat = jnp.swapaxes(normed[...], 0, 1).reshape(windows * half * WIN, width).astype(BF16)
        scale = jnp.float32(1.0 / math.sqrt(width // HEADS))

        @pl.loop(0, 3 * width // 256)
        def _(n):
            on = pl.ds(pl.multiple_of(n * 256, 256), 256)
            value = jnp.dot(flat, wqkv[:, on], preferred_element_type=F32).astype(BF16)
            value = (value.astype(F32) * jnp.where(n < width // 256, scale, 1.0)).astype(BF16)
            qkv_out[:, at, on] = value.reshape(windows, half * WIN, 256)

    def attend(qkv_in, cells, bias):
        head = width // HEADS
        pair = 2 * head
        lanes = lax.broadcasted_iota(jnp.int32, (cells, pair), 1) < head

        @pl.loop(0, windows, unroll=2)
        def _(w):
            for group in range(0, HEADS // 2, 4):
                spots = [p * pair for p in range(group, group + 4)]
                scores = []
                for on in spots:
                    qp = qkv_in[w, :, on : on + pair]
                    zero = jnp.zeros_like(qp)
                    q2 = jnp.concatenate([jnp.where(lanes, qp, zero), jnp.where(lanes, zero, qp)], axis=0)
                    kp = qkv_in[w, :, width + on : width + on + pair]
                    s = lax.dot_general(q2, kp, NT, preferred_element_type=F32)
                    scores.append(s if bias is None else s + bias)
                peaks = [jnp.max(s, axis=-1, keepdims=True) for s in scores]
                powers = [jnp.exp(s - m).astype(BF16) for s, m in zip(scores, peaks)]
                mixed = []
                for on, e in zip(spots, powers):
                    vp = qkv_in[w, :, 2 * width + on : 2 * width + on + pair]
                    ones = jnp.ones_like(vp)
                    low_out = jnp.dot(e[:cells], jnp.where(lanes, vp, ones), preferred_element_type=F32)
                    high_out = jnp.dot(e[cells:], jnp.where(lanes, ones, vp), preferred_element_type=F32)
                    total = pltpu.roll(jnp.where(lanes, high_out, low_out), head, 1)
                    mixed.append((jnp.where(lanes, low_out, high_out) / total).astype(BF16))
                att[w, 0:cells, spots[0] : spots[0] + 4 * pair] = jnp.concatenate(mixed, axis=1)

    def decode(at, x_in, outs):
        mixed = att[:, at, :].reshape(windows * half * WIN, width)

        @pl.loop(0, width // 256)
        def _(n):
            on = pl.ds(pl.multiple_of(n * 256, 256), 256)
            update = jnp.dot(mixed, wo[:, on], preferred_element_type=F32)
            update = jnp.swapaxes(update.reshape(windows, half, WIN, 256), 0, 1)
            value = x_in[:, :, :, on] + update
            lo[:, on] = value.reshape(half * cols, 256).astype(BF16)

        value = lax.dot_general(wdt[...], lo[...], NT, preferred_element_type=F32).astype(BF16)
        for chosen_here, out in outs:
            if chosen_here is None:
                out[...] = value
            else:

                @pl.when(chosen_here)
                def _():
                    out[...] = value

    top_at, own_at = slice(0, half * WIN), slice(half * WIN, 2 * half * WIN)
    x_top, x_own = xs.at[0], xs.at[1]
    own_load.wait()
    edge_copy.wait()
    loads[0].wait()
    loads[1].wait()
    project(own.at[pl.ds(0, half)], edge.at[pl.ds(0, half)], x_own, qkv, own_at)

    loads[2].wait()
    loads[3].wait()
    patches = wdt.shape[0]
    row_id = lax.broadcasted_iota(jnp.int32, (patches, patches), 0)
    col_id = lax.broadcasted_iota(jnp.int32, (patches, patches), 1)
    area = PATCH * PATCH
    wanted = (row_id % channels) * area + (row_id // channels) % PATCH * PATCH + row_id // (PATCH * channels)
    chosen = (col_id == wanted).astype(F32).astype(BF16)
    wdt[...] = lax.dot_general(chosen, wd[...], NT, preferred_element_type=F32).astype(BF16)

    @pl.when(lat == n_lat - 1)
    def _():
        project(own.at[pl.ds(half, half)], edge.at[pl.ds(half, half)], xs_b, qkv_b, top_at)

    for starts, source, tables in zip(block_starts(length), (rows1_ref, rows4_ref), ((high, low), (dhigh, dlow))):
        bases = sorted({start % 128 for start in starts})
        for g, start in enumerate(starts):
            cut = length - start // 128 * 128
            for j in range(2):
                value = source[j, bases.index(start % 128)]
                if cut < length:
                    value = jnp.concatenate([value[:, cut:], value[:, :cut]], axis=1)
                tables[j][16 * g : 16 * g + 16, :] = value

    eye = lax.broadcasted_iota(jnp.int32, (channels, channels), 0)
    eye = eye == lax.broadcasted_iota(jnp.int32, (channels, channels), 1)
    strength[...] = jnp.sum(jnp.where(eye, nudge_ref[...], 0.0), axis=1, keepdims=True)

    own_state.wait()
    state_copy.wait()

    @pl.loop(0, channels // LEV)
    def _(g):
        on = pl.ds(pl.multiple_of(g * LEV, LEV), LEV)
        s = band[on].reshape(LEV * tall, length)
        s_high, s_low = split(s)
        kept = jnp.dot(s_high, high[...], preferred_element_type=F32)
        kept = kept + jnp.dot(s_low, high[...], preferred_element_type=F32)
        kept = kept + jnp.dot(s_high, low[...], preferred_element_type=F32)
        kept = s.reshape(LEV, tall, length) - strength[on][:, :, None] * kept.reshape(LEV, tall, length)
        base[:, on, :] = jnp.swapaxes(kept, 0, 1)

    @pl.when(lat == 0)
    def _():
        recv[...] = jnp.zeros_like(recv)

    @pl.when(has_prev)
    def _():
        row_a.wait_recv()

    corner_copy.start()

    @pl.when(has_prev)
    def _():
        row_b.wait_recv()

    corner_copy.wait()
    project(recv, corner, x_top, qkv, top_at)
    key = lax.broadcasted_iota(jnp.int32, (1, 2 * half * WIN), 1)
    bias = jnp.where((key < half * WIN) & (lat == 0), -1e30, 0.0).astype(F32)
    attend(qkv, 2 * half * WIN, bias)

    top_copies = [remote(5 + j, send_top, d, prev, 1) for j, d in enumerate((d0, d1))]
    side_high = is_low & (lat == n_lat - 1)

    decode(top_at, x_top, [(None, send_top)])
    for j in range(2):

        @pl.when(has_prev & (lon == j))
        def _():
            top_copies[j].start()

    decode(own_at, x_own, [(is_high, send_side), (is_low, d0)])

    @pl.when(is_high)
    def _():
        to_low_now = remote(8, send_side, d1, lat, 0)
        to_low_now.start()

    @pl.when(lat == n_lat - 1)
    def _():
        attend(qkv_b, half * WIN, None)
        decode(top_at, xs_b, [(is_high, d1), (is_low, send_side)])

    @pl.when(side_high)
    def _():
        to_high_last = remote(7, send_side, d0, lat, 1)
        to_high_last.start()

    @pl.when(is_low)
    def _():
        remote(8, send_side, d1, lat, peer).wait_recv()

    @pl.when(is_high & has_next)
    def _():
        remote(5, send_top, d0, prev, 1).wait_recv()
        remote(6, send_top, d1, prev, 1).wait_recv()

    @pl.when(is_high & (lat == n_lat - 1))
    def _():
        remote(7, send_side, d0, lat, peer).wait_recv()

    part = PATCH * channels

    def nudge_rows(r):
        pieces = []
        for b in range(PATCH):
            for d in (d0, d1):
                pieces.append(d[b * part : (b + 1) * part, r * cols : (r + 1) * cols])
        x = jnp.concatenate(pieces, axis=1)
        kept = jnp.dot(x, dhigh[...], preferred_element_type=F32)
        kept = kept + jnp.dot(x, dlow[...], preferred_element_type=F32)
        y = r * PATCH
        base[y : y + PATCH] = base[y : y + PATCH] + strength[...][None] * kept.reshape(PATCH, channels, length)

    up_lat, up_lon = jnp.where(is_low, lat, nxt), peer
    down_lat, down_lon = jnp.where(is_low, prev, lat), peer
    inside_up, inside_down = is_low | has_next, is_high | has_prev
    up_copy = remote(9, up_rows, before, up_lat, up_lon)
    down_copy = remote(10, down_rows, after, down_lat, down_lon)
    count = tall // PATCH
    nudge_rows(count - 1)
    up_rows[...] = base[tall - 2 : tall].astype(BF16)

    @pl.when(inside_up)
    def _():
        up_copy.start()

    nudge_rows(0)
    down_rows[...] = base[0:2].astype(BF16)

    @pl.when(inside_down)
    def _():
        down_copy.start()

    for r in range(1, count - 1):
        nudge_rows(r)

    def row(y):
        if y < 0:
            return before[y + 2].astype(F32)
        if y >= tall:
            return after[y - tall].astype(F32)
        return base[y]

    def section(y):
        first[y + 1] = row(y) + time_step * tendency_row(row(y - 1), row(y), row(y + 1))

    @pl.loop(1, tall - 1)
    def _(y):
        first[y + 1] = base[y] + time_step * tendency_row(base[y - 1], base[y], base[y + 1])

    @pl.when(inside_down)
    def _():
        up_copy.wait_recv()

    @pl.when(jnp.logical_not(inside_down))
    def _():
        before[...] = jnp.zeros_like(before)

    @pl.when(inside_up)
    def _():
        down_copy.wait_recv()

    @pl.when(jnp.logical_not(inside_up))
    def _():
        after[...] = jnp.zeros_like(after)

    for y in (-1, 0, tall - 1, tall):
        section(y)
    first[0] = first[0] * jnp.where(inside_down, 1.0, 0.0)
    first[tall + 1] = first[tall + 1] * jnp.where(inside_up, 1.0, 0.0)

    @pl.loop(0, tall)
    def _(y):
        second = tendency_row(first[y], first[y + 1], first[y + 2])
        base[y] = 0.5 * (base[y] + first[y + 1] + time_step * second)

    for g in range(0, tall, 8):
        out_ref[:, g : g + 8, :] = jnp.swapaxes(base[g : g + 8], 0, 1)

    @pl.when(has_next)
    def _():
        row_a.wait_send()
        row_b.wait_send()

    for j in range(2):

        @pl.when(has_prev & (lon == j))
        def _():
            top_copies[j].wait_send()

    @pl.when(side_high)
    def _():
        remote(7, send_side, d0, lat, 1).wait_send()

    @pl.when(is_high)
    def _():
        remote(8, send_side, d1, lat, 0).wait_send()

    @pl.when(inside_up)
    def _():
        up_copy.wait_send()

    @pl.when(inside_down)
    def _():
        down_copy.wait_send()


def body(sizes, tokens, ln_gain, w_query, w_keyval, w_out, w_dec, nudge, state):
    half = WIN // 2
    cols, width = tokens.shape[1:]
    channels = nudge.shape[0]
    length = state.shape[2] * sizes["lon"]
    tall = state.shape[1] // sizes["lon"]
    windows = cols // WIN
    patches = w_dec.shape[1]
    strip = 16
    cells = half * WIN
    hbm, vmem = pl.BlockSpec(memory_space=pl.ANY), pl.BlockSpec(memory_space=pltpu.VMEM)
    V = pltpu.VMEM
    field = (tall, channels, length)
    flow = (patches, half * cols)
    scratch = [
        V((width, 3 * width), BF16), V((width, width), BF16), V(w_dec.shape, BF16), V((patches, width), BF16),
        V(tokens.shape, BF16), V((half, cols, width), BF16), V((2 * half, strip, width), BF16),
        V((half, strip, width), BF16),
        V((2, half, windows, WIN, width), F32), V((half, windows, WIN, width), F32),
        V((half, windows, WIN, width), F32),
        V((windows, 2 * cells, 3 * width), BF16), V((windows, cells, 3 * width), BF16),
        V((windows, 2 * cells, width), BF16), V((half * cols, width), BF16),
        V((channels, tall, length), F32), V(field, F32),
        V((length, length), BF16), V((length, length), BF16), V((length, length), BF16), V((length, length), BF16),
        V(flow, BF16), V(flow, BF16), V(flow, BF16), V(flow, BF16),
        V((2, channels, length), BF16), V((2, channels, length), BF16),
        V((2, channels, length), BF16), V((2, channels, length), BF16),
        V((tall + 2, channels, length), F32), V((channels, 1), F32),
        pltpu.SemaphoreType.DMA((6,)), pltpu.SemaphoreType.DMA((11,)), pltpu.SemaphoreType.DMA((11,)),
    ]
    tables = [
        filter_rows(length, KEEP, stride, sorted({start % 128 for start in starts}))
        for stride, starts in zip((1, PATCH), block_starts(length))
    ]
    advanced = pl.pallas_call(
        functools.partial(cycle_kernel, sizes["lat"]),
        out_shape=jax.ShapeDtypeStruct((channels, tall, length), F32),
        in_specs=[hbm] * 6 + [vmem] * 4,
        out_specs=vmem,
        scratch_shapes=scratch,
        compiler_params=pltpu.CompilerParams(
            collective_id=0, has_side_effects=True, vmem_limit_bytes=62 * 2**20
        ),
        name="cycle",
    )(
        tokens, state, w_query, w_keyval, w_out, w_dec, ln_gain[None], nudge[None],
        *tables,
    )
    return advanced


def tendency_row(south, centre, north):
    channels, length = centre.shape
    west = pltpu.roll(centre, 1, 1)
    east = pltpu.roll(centre, length - 1, 1)
    u = centre[:LEV][None]
    v = centre[LEV : 2 * LEV][None]
    dx = (east - west).reshape(VARS, LEV, length)
    dy = (north - south).reshape(VARS, LEV, length)
    advection = ((u * dx + v * dy) * 0.5).reshape(channels, length)
    return diffusion * (east + west + north + south - 4.0 * centre) - advection


def solution(mesh):
    in_specs = (
        P(("member", "lat"), "lon", None),
        P(),
        P(),
        P(),
        P(),
        P(),
        P(),
        P(None, ("member", "lat"), "lon"),
    )
    out_specs = P(None, ("member", "lat", "lon"), None)
    return jax.shard_map(
        functools.partial(body, dict(mesh.shape)),
        mesh=mesh,
        in_specs=in_specs,
        out_specs=out_specs,
        check_vma=False,
    )
```
